1024 devices in a mesh: seq: 64 (over y, x), head: 16 (over z, core).
Axes of the slice: x: 8, y: 8, z: 8, core: 2. Of those that a mesh axis runs over, the one named last changes fastest.
Arguments:
- lin_qkv: bfloat16 [16384, 3, 4096], P('seq', None, 'head'), may hold values from -6 to 6
- resid: bfloat16 [16384, 4096], P('seq', 'head'), may hold values from -6 to 6
- w_out: bfloat16 [4096, 4096], P('head'), may hold values from -0.125 to 0.125
- w_qkv: bfloat16 [4096, 3, 4096], P(None, None, 'head'), may hold values from -2 to 2
Outputs:
- hidden: bfloat16 [16384, 4096], P('seq', 'head')
- attended: bfloat16 [16384, 4096], P('seq', 'head')
The draws below stay inside these ranges and needn't reach their ends.
All inputs are finite; a program needn't handle non-finite values.
Results may differ from the reference program's by a relative error of at most 0.025.
Values may be sent and summed in bfloat16 or wider, within the bound.
A program may use at most 64 MiB of HBM per device.

```python
import math
import jax
import jax.numpy as jnp
from jax import lax

D = 4096
HEADS = 32
HD = 128
TOK_DEV = 256
TOKENS = 16384
N_SEQ = 64


def draw_w_qkv(key, part):
    limit = 6.0 / math.sqrt(D)
    base = jnp.clip(jax.random.normal(key, (D, 3, HEADS * HD), jnp.float32) / math.sqrt(D), -limit, limit)
    return base.astype(jnp.bfloat16)


def with_spikes(values, stream_key, source, target, blocks, factor):
    def block_of(position):
        return (jnp.arange(values.shape[position]) // (values.shape[position] // blocks)).reshape((-1,) + (1,) * (values.ndim - 1 - position))

    first = jax.random.permutation(stream_key, blocks)[block_of(target)]
    second = (block_of(target) + blocks // 2) % blocks
    return jnp.where((block_of(source) == first) | (block_of(source) == second), factor * values, values)


def steps_of(key, dims, shards, smallest, largest):
    level, own = 1.0, jax.random.fold_in(key, 6)
    for position, blocks in shards:
        draws = jnp.exp(jax.random.uniform(jax.random.fold_in(own, position), (blocks,), jnp.float32, smallest / len(shards), largest / len(shards)))
        level = level * jnp.repeat(draws, dims[position] // blocks).reshape([-1 if axis == position else 1 for axis in range(len(dims))])
    return level


def scatter_about(rng, extent, scale, most, split=(), kind=jnp.bfloat16):
    entries = scale * jax.random.normal(rng, extent, jnp.float32)
    if split:
        entries = entries * steps_of(rng, extent, split, -0.22, 0.18)
    return jnp.clip(entries, -most, most).astype(kind)


def heavy_noise(rng, dims, scale, most, split, heavy, kind=jnp.bfloat16):
    result = scale * jax.random.normal(rng, dims, jnp.float32)
    if split:
        result = result * steps_of(rng, dims, split, -0.22, 0.18)
    return jnp.clip(with_spikes(result, jax.random.fold_in(rng, 3), *heavy), -most, most).astype(kind)


def setup_inputs(seed: int = 0) -> dict:
    splits = jax.random.split(jax.random.key(seed), 5)
    return {
        "lin_qkv": scatter_about(splits[0], (TOKENS, 3, HEADS * HD), 1.0, 6.0, ((0, 64), (2, 16))),
        "resid": scatter_about(splits[1], (TOKENS, D), 1.0, 6.0, ((0, 64), (1, 16))),
        "w_out": heavy_noise(splits[2], (HEADS * HD, D), (HEADS * HD) ** -0.5, 0.125, ((0, 16),), (0, 1, 16, 2.0)),
        "w_qkv": draw_w_qkv(jax.random.fold_in(splits[4], 71), 0),
    }


def rotary(values, positions):
    half = HD // 2
    freq = 500000.0 ** (-(jnp.arange(half, dtype=jnp.float32) * 2.0 / HD))
    angle = positions.astype(jnp.float32)[:, None] * freq[None, :]
    cosine = jnp.cos(angle)[:, None, :]
    sine = jnp.sin(angle)[:, None, :]
    first = values[..., :half]
    second = values[..., half:]
    return jnp.concatenate([first * cosine - second * sine, second * cosine + first * sine], axis=-1)

def reference(lin_qkv, resid, w_out, w_qkv):
    blocks = lin_qkv.reshape(N_SEQ, TOK_DEV, 3, HEADS, HD)

    def kv_state(block):
        keys = block[:, 1].astype(jnp.float32)
        values = block[:, 2].astype(jnp.float32)
        return jnp.einsum('thd,the->hde', keys, values)
    states = lax.map(kv_state, blocks)
    running = jnp.cumsum(states, axis=0)
    prefix = jnp.concatenate([jnp.zeros_like(states[:1]), running[:-1]], axis=0).astype(jnp.bfloat16)
    scale = 1.0 / math.sqrt(HD * TOKENS)
    causal = jnp.tril(jnp.ones((TOK_DEV, TOK_DEV), dtype=bool))

    def lin_block(items):
        block, before = items
        queries = block[:, 0].astype(jnp.float32)
        keys = block[:, 1].astype(jnp.float32)
        values = block[:, 2].astype(jnp.float32)
        scores = jnp.einsum('thd,shd->hts', queries, keys)
        inner = jnp.where(causal[None], scores, 0.0).astype(jnp.bfloat16)
        inner = lax.optimization_barrier(inner).astype(jnp.float32)
        total = jnp.einsum('hts,shd->thd', inner, values) + jnp.einsum('thd,hde->the', queries, before.astype(jnp.float32))
        return (total * scale).astype(jnp.bfloat16)
    lin_out = lax.map(lin_block, (blocks, prefix)).reshape(TOKENS, HEADS * HD)
    mixed_f = resid.astype(jnp.float32) + jnp.dot(lin_out, w_out, preferred_element_type=jnp.float32)
    hidden = mixed_f.astype(jnp.bfloat16)
    meansq = lax.optimization_barrier(jnp.sum(mixed_f * mixed_f, axis=1, keepdims=True)) / D
    normed = (mixed_f * lax.rsqrt(meansq + 1e-05)).astype(jnp.bfloat16)
    proj = jnp.dot(normed, w_qkv.reshape(D, 3 * HEADS * HD), preferred_element_type=jnp.float32)
    proj = proj.reshape(TOKENS, 3, HEADS, HD)
    positions = jnp.arange(TOKENS, dtype=jnp.int32)
    query2 = rotary(proj[:, 0], positions).astype(jnp.bfloat16).reshape(N_SEQ, TOK_DEV, HEADS, HD)
    key2 = rotary(proj[:, 1], positions).astype(jnp.bfloat16).reshape(N_SEQ, TOK_DEV, HEADS, HD)
    value2 = proj[:, 2].astype(jnp.bfloat16).reshape(N_SEQ, TOK_DEV, HEADS, HD)
    key_prev = jnp.concatenate([jnp.zeros_like(key2[:1]), key2[:-1]], axis=0)
    value_prev = jnp.concatenate([jnp.zeros_like(value2[:1]), value2[:-1]], axis=0)
    score_scale = 1.0 / math.sqrt(HD)

    def soft_block(items):
        queries, kprev, vprev, kown, vown, number = items
        keys = jnp.concatenate([kprev, kown], axis=0).astype(jnp.float32)
        values = jnp.concatenate([vprev, vown], axis=0).astype(jnp.float32)
        scores = jnp.einsum('thd,shd->hts', queries.astype(jnp.float32), keys) * score_scale
        allowed = jnp.concatenate([jnp.full((TOK_DEV, TOK_DEV), number > 0), causal], axis=1)
        scores = jnp.where(allowed[None], scores, -1e+30)
        top = lax.optimization_barrier(jnp.max(scores, axis=2, keepdims=True))
        expo = jnp.where(allowed[None], jnp.exp(scores - top), 0.0)
        probs = expo / lax.optimization_barrier(jnp.sum(expo, axis=2, keepdims=True))
        weights = lax.optimization_barrier(probs.astype(jnp.bfloat16)).astype(jnp.float32)
        return jnp.einsum('hts,shd->thd', weights, values).astype(jnp.bfloat16)
    numbers = jnp.arange(N_SEQ, dtype=jnp.int32)
    attended = lax.map(soft_block, (query2, key_prev, value_prev, key2, value2, numbers))
    return (hidden, attended.reshape(TOKENS, HEADS * HD))
```

```python
import functools
import math

import jax
import jax.numpy as jnp
import numpy as np
from jax import lax
from jax.experimental import pallas as pl
from jax.experimental.pallas import tpu as pltpu
from jax.sharding import Mesh
from jax.sharding import PartitionSpec as P

HD = 128
BF = jnp.bfloat16
F32 = jnp.float32
MESH_ID = pl.DeviceIdType.MESH


def dot(a, b, contract=(1, 0)):
    dims = (((contract[0],), (contract[1],)), ((), ()))
    return lax.dot_general(a, b, dims, preferred_element_type=F32)


def remote(src, dst, send, recv, **where):
    return pltpu.make_async_remote_copy(
        src_ref=src, dst_ref=dst, send_sem=send, recv_sem=recv, device_id=where, device_id_type=MESH_ID
    )


def far_first(n):
    return sorted(range(1, n), key=lambda k: -min(k, n - k))


def layer_pair(
    sizes,
    scale,
    qkv_hbm,
    resid_hbm,
    wo_hbm,
    wq_hbm,
    near_hbm,
    far_hbm,
    hidden_ref,
    attended_ref,
    qkv,
    resid,
    w2,
    wq,
    near,
    far,
    st,
    p1,
    totals,
    p3s,
    p3,
    loc,
    lin2,
    part,
    out_r,
    in_r,
    out_l,
    in_l,
    hg,
    acc,
    sumsq,
    kv,
    kvp,
    load_sem,
    wo_sem,
    wx_send,
    wx_recv,
    s1,
    r1,
    s2,
    r2,
    s3,
    r3,
    lin_send,
    lin_recv,
    rr_send,
    rr_recv,
    rl_send,
    rl_recv,
    gr_send,
    gr_recv,
    gl_send,
    gl_recv,
    gc_send,
    gc_recv,
    kv_send,
    kv_recv,
):
    ny, nx, nz = sizes
    half_z = nz // 2
    y, x, z, c = (lax.axis_index(name) for name in ("y", "x", "z", "c"))
    tok, width = resid.shape
    half = tok // 2
    halves = (pl.ds(0, half), pl.ds(half, half))
    heads = (pl.ds(0, HD), pl.ds(HD, HD))
    other = 1 - c
    right, left = lax.rem(z + 1, nz), lax.rem(z + nz - 1, nz)
    next_x = lax.rem(x + 1, nx)
    next_y = lax.rem(y + (x + 1) // nx, ny)
    prev_x = lax.rem(x + nx - 1, nx)
    prev_y = lax.rem(y + ny - 1 + (x + nx - 1) // nx, ny)
    block = y * nx + x

    load_qkv = pltpu.make_async_copy(qkv_hbm, qkv, load_sem.at[0])
    load_qkv.start()
    barrier = pltpu.get_barrier_semaphore()
    greeted = 0
    places = [{"x": lax.rem(x + k, nx)} for k in range(1, nx)]
    places += [{"y": lax.rem(y + k, ny)} for k in range(1, ny)]
    places += [{"z": right}, {"z": left}, {"c": other}]
    places += [{"y": next_y, "x": next_x}, {"y": prev_y, "x": prev_x}]
    for place in places:
        pl.semaphore_signal(barrier, inc=1, device_id=place, device_id_type=MESH_ID)
        greeted += 1

    load_qkv.wait()
    for h in range(2):
        state = dot(qkv[1, :, heads[h]], qkv[2, :, heads[h]], (0, 0)).astype(BF)
        st[pl.ds(h * nx // 2, nx // 2)] = state.reshape(nx // 2, -1, HD)
    pl.semaphore_wait(barrier, greeted)

    def to_x(k):
        there = lax.rem(x + k, nx)
        return remote(st.at[there], p1.at[x], s1.at[k], r1.at[k], x=there)

    def from_x(k):
        there = lax.rem(x + nx - k, nx)
        return remote(st.at[there], p1.at[there], s1.at[k], r1.at[k], x=there)

    for k in far_first(nx):
        to_x(k).start()
    loads = [
        pltpu.make_async_copy(resid_hbm, resid, load_sem.at[1]),
        pltpu.make_async_copy(near_hbm, near, load_sem.at[2]),
        pltpu.make_async_copy(far_hbm, far, load_sem.at[3]),
        pltpu.make_async_copy(wq_hbm, wq, load_sem.at[4]),
    ]

    def wo_block(j, core):
        return wo_hbm.at[:, pl.ds(pl.multiple_of((2 * j + core) * width, width), width)]

    def wo_own(j):
        return pltpu.make_async_copy(wo_block(j, c), w2.at[j, c], wo_sem.at[j])

    def wo_swap(j, slot):
        return remote(wo_block(j, other), w2.at[j, slot], wx_send.at[j], wx_recv.at[j], c=other)

    for j in range(nz):
        wo_own(j).start()
        wo_swap(j, c).start()
    for load in loads:
        load.start()

    p1[pl.ds(x, 1)] = st[pl.ds(x, 1)]
    rows = lax.broadcasted_iota(jnp.int32, (tok, tok), 0)
    cols = lax.broadcasted_iota(jnp.int32, (tok, tok), 1)
    causal = cols <= rows
    for h in range(2):
        scores = dot(qkv[0, :, heads[h]], qkv[1, :, heads[h]], (1, 1))
        inner = jnp.where(causal, scores, 0.0).astype(BF)
        loc[:, heads[h]] = dot(inner, qkv[2, :, heads[h]])

    for k in far_first(nx)[::-1]:
        from_x(k).wait_recv()
    row_total = p1[0].astype(F32)
    for j in range(1, nx):
        row_total = row_total + p1[j].astype(F32)
    totals[pl.ds(y, 1)] = row_total.astype(BF)[None]

    def to_y(k):
        there = lax.rem(y + k, ny)
        return remote(totals.at[y], totals.at[y], s2.at[k], r2.at[k], y=there)

    def from_y(k):
        there = lax.rem(y + ny - k, ny)
        return remote(totals.at[there], totals.at[there], s2.at[k], r2.at[k], y=there)

    for k in far_first(ny):
        to_y(k).start()

    loads[1].wait()
    loads[2].wait()
    far_cos, far_sin = far[0, pl.ds(block, 1), :], far[1, pl.ds(block, 1), :]
    near_cos, near_sin = near[0], near[1]
    lane = lax.broadcasted_iota(jnp.int32, (tok, HD), 1)
    cosine = far_cos * near_cos - far_sin * near_sin
    sine = far_sin * near_cos + far_cos * near_sin
    near[0] = cosine
    near[1] = jnp.where(lane < HD // 2, -sine, sine)

    for k in far_first(ny)[::-1]:
        from_y(k).wait_recv()
    running = jnp.zeros_like(row_total)
    for j in range(ny):
        running = running + jnp.where(j < y, totals[j].astype(F32), 0.0)
    for j in range(nx):
        p3s[j] = running.astype(BF)
        running = running + p1[j].astype(F32)

    def back_x(k):
        there = lax.rem(x + k, nx)
        return remote(p3s.at[there], p3.at[x], s3.at[k], r3.at[k], x=there)

    def got_x(k):
        there = lax.rem(x + nx - k, nx)
        return remote(p3s.at[there], p3.at[there], s3.at[k], r3.at[k], x=there)

    for k in far_first(nx):
        back_x(k).start()
    p3[pl.ds(x, 1)] = p3s[pl.ds(x, 1)]
    for j in range(nz):
        wo_own(j).wait()
        wo_swap(j, other).wait_recv()
    loads[0].wait()
    for k in far_first(nx)[::-1]:
        got_x(k).wait_recv()

    for h in range(2):
        before = p3[pl.ds(h * nx // 2, nx // 2)].reshape(HD, HD)
        total = loc[:, heads[h]] + dot(qkv[0, :, heads[h]], before)
        lin2[c, :, heads[h]] = (total * scale).astype(BF)

    def lin_swap(slot):
        return remote(lin2.at[c], lin2.at[slot], lin_send, lin_recv, c=other)

    lin_swap(c).start()

    def own_part(j, _):
        part[j] = dot(lin2[c], w2[j, c])
        return 0

    lax.fori_loop(0, nz, own_part, 0)
    lin_swap(other).wait_recv()

    def at(k):
        return lax.rem(z + k + nz, nz)

    def finish_part(k):
        j = at(k)
        part[j] = part[j] + dot(lin2[other], w2[j, other])

    def ring_r(s, h):
        return remote(out_r.at[s, h], in_r.at[s, h], rr_send.at[s, h], rr_recv.at[s, h], z=right)

    def ring_l(s, h):
        return remote(out_l.at[s, h], in_l.at[s, h], rl_send.at[s, h], rl_recv.at[s, h], z=left)

    def pass_r(s, h, first):
        value = part[at(half_z - s), halves[h]]
        if not first:
            ring_r(s - 1, h).wait_recv()
            value = value + in_r[s - 1, h].astype(F32)
        out_r[s, h] = value.astype(BF)
        ring_r(s, h).start()

    def pass_l(s, h, first):
        value = part[at(s - half_z), halves[h]]
        if not first:
            ring_l(s - 1, h).wait_recv()
            value = value + in_l[s - 1, h].astype(F32)
        out_l[s, h] = value.astype(BF)
        ring_l(s, h).start()

    finish_part(half_z)
    pass_r(0, 0, True)
    pass_l(0, 1, True)
    finish_part(half_z - 1)
    pass_r(1, 1, True)
    finish_part(1 - half_z)
    pass_l(1, 0, True)
    for k in range(half_z - 2, 0, -1):
        finish_part(k)
        finish_part(-k)
    finish_part(0)
    pass_r(1, 0, False)
    pass_l(1, 1, False)
    for s in range(2, half_z):
        pass_r(s, 1, False)
        pass_l(s, 0, False)
        pass_r(s, 0, False)
        pass_l(s, 1, False)

    last = half_z - 1
    acc[...] = jnp.zeros_like(acc)
    sumsq[...] = jnp.zeros_like(sumsq)

    def gather_r(s, h):
        return hg.at[at(-s), c, halves[h]]

    def gather_l(s, h):
        return hg.at[at(s), c, halves[h]]

    def send_r(s, h):
        return remote(gather_r(s, h), gather_r(s, h), gr_send.at[s, h], gr_recv.at[s, h], z=right)

    def send_l(s, h):
        return remote(gather_l(s, h), gather_l(s, h), gl_send.at[s, h], gl_recv.at[s, h], z=left)

    def got_r(s, h):
        return remote(gather_r(s + 1, h), gather_r(s + 1, h), gr_send.at[s, h], gr_recv.at[s, h], z=right)

    def got_l(s, h):
        return remote(gather_l(s + 1, h), gather_l(s + 1, h), gl_send.at[s, h], gl_recv.at[s, h], z=left)

    def to_core(k, h):
        piece = hg.at[at(k), c, halves[h]]
        slot = lax.rem(k + nz, nz)
        return remote(piece, piece, gc_send.at[slot, h], gc_recv.at[slot, h], c=other)

    def from_core(k, h):
        piece = hg.at[at(k), other, halves[h]]
        slot = lax.rem(k + nz, nz)
        return remote(piece, piece, gc_send.at[slot, h], gc_recv.at[slot, h], c=other)

    for h in (0, 1):
        if h == 0:
            ring_l(last, 0).wait_recv()
            ring_r(last, 0).wait_recv()
        else:
            ring_r(last, 1).wait_recv()
            ring_l(last, 1).wait_recv()
        mixed = resid[halves[h], :].astype(F32) + part[z, halves[h]]
        mixed = mixed + in_r[last, h].astype(F32) + in_l[last, h].astype(F32)
        mixed = mixed.astype(BF)
        hg[z, c, halves[h]] = mixed
        send_r(0, h).start()
        send_l(0, h).start()
        to_core(0, h).start()
        hidden_ref[halves[h], :] = mixed
    loads[3].wait()

    def project(k, core):
        j = at(k)
        values = hg[j, core]
        rows_of = pl.ds(pl.multiple_of((2 * j + core) * width, width), width)
        for i in range(3):
            acc[i] += dot(values, wq[i, rows_of, :])
        wide = values.astype(F32)
        squares = wide * wide
        sumsq[...] += squares[:, :HD] + squares[:, HD:]

    def project_other(k):
        from_core(k, 0).wait_recv()
        from_core(k, 1).wait_recv()
        project(k, other)

    project(0, c)

    def gather_step(s, _):
        got_r(s, 0).wait_recv()

        @pl.when(s < last)
        def _():
            send_r(s + 1, 0).start()

        got_l(s, 1).wait_recv()

        @pl.when(s < last)
        def _():
            send_l(s + 1, 1).start()

        to_core(-1 - s, 0).start()
        to_core(s + 1, 1).start()

        @pl.when(s < last)
        def _():
            got_r(s, 1).wait_recv()

            @pl.when(s < last - 1)
            def _():
                send_r(s + 1, 1).start()

            got_l(s, 0).wait_recv()

            @pl.when(s < last - 1)
            def _():
                send_l(s + 1, 0).start()

            to_core(-1 - s, 1).start()
            to_core(s + 1, 0).start()

        project(-1 - s, c)

        @pl.when(s < last)
        def _():
            project(s + 1, c)

        @pl.when(s == 0)
        def _():
            project_other(0)

        @pl.when(s > 0)
        def _():
            project_other(-s)
            project_other(s)

        return 0

    lax.fori_loop(0, half_z, gather_step, 0)
    project_other(half_z)

    mean = jnp.sum(sumsq[...], axis=1, keepdims=True) / (width * 2 * nz)
    row_scale = lax.rsqrt(mean + 1e-05)

    def rotated(i, h):
        values = acc[i, :, heads[h]] * row_scale
        return (values * near[0] + pltpu.roll(values, HD // 2, 1) * near[1]).astype(BF)

    def kv_copy(i):
        return remote(kv.at[i], kvp.at[i], kv_send.at[i], kv_recv.at[i], y=next_y, x=next_x)

    for h in range(2):
        kv[0, :, heads[h]] = rotated(1, h)
    kv_copy(0).start()
    kv[1] = (acc[2] * row_scale).astype(BF)
    kv_copy(1).start()

    score_scale = 1.0 / math.sqrt(HD)
    queries, tops, sums, outs = [], [], [], []
    for h in range(2):
        q = rotated(0, h)
        logits = jnp.where(causal, dot(q, kv[0, :, heads[h]], (1, 1)) * score_scale, -1e30)
        top = jnp.max(logits, axis=1, keepdims=True)
        expo = jnp.exp(logits - top)
        queries.append(q)
        tops.append(top)
        sums.append(jnp.sum(expo, axis=1, keepdims=True))
        outs.append(dot(expo.astype(BF), kv[1, :, heads[h]]))
    kv_copy(0).wait_recv()
    weights = []
    for h in range(2):
        logits = dot(queries[h], kvp[0, :, heads[h]], (1, 1)) * score_scale
        logits = jnp.where(block > 0, logits, -1e30)
        top = jnp.maximum(tops[h], jnp.max(logits, axis=1, keepdims=True))
        expo = jnp.exp(logits - top)
        old = jnp.exp(tops[h] - top)
        sums[h] = sums[h] * old + jnp.sum(expo, axis=1, keepdims=True)
        outs[h] = outs[h] * old
        weights.append(expo.astype(BF))
    kv_copy(1).wait_recv()
    for h in range(2):
        out = outs[h] + dot(weights[h], kvp[1, :, heads[h]])
        attended_ref[:, heads[h]] = (out / sums[h]).astype(BF)

    for k in range(1, nx):
        to_x(k).wait_send()
        back_x(k).wait_send()
    for k in range(1, ny):
        to_y(k).wait_send()
    for j in range(nz):
        wo_swap(j, c).wait_send()
    lin_swap(c).wait_send()
    for s in range(half_z):
        for h in range(2):
            if s or h == 0:
                ring_r(s, h).wait_send()
            if s or h == 1:
                ring_l(s, h).wait_send()
            if s < last or h == 0:
                send_r(s, h).wait_send()
            if s < last or h == 1:
                send_l(s, h).wait_send()
    for k in range(nz):
        for h in range(2):
            to_core(k, h).wait_send()
    for i in range(2):
        kv_copy(i).wait_send()


def tables(tok, blocks):
    freq = 500000.0 ** (-(np.arange(HD // 2) * 2.0 / HD))
    freq = np.concatenate([freq, freq])
    near = np.arange(tok)[:, None] * freq
    far = (np.arange(blocks) * tok)[:, None] * freq
    return tuple(np.stack([np.cos(a), np.sin(a)]).astype(np.float32) for a in (near, far))


def local(sizes, lin_qkv, resid, w_out, w_qkv):
    ny, nx, nz = sizes
    tok, width = resid.shape
    half_z = nz // 2
    near, far = tables(tok, ny * nx)
    scale = 1.0 / math.sqrt(HD * tok * ny * nx)
    rows = 2 * HD // nx
    anywhere = pl.BlockSpec(memory_space=pl.ANY)
    dma = pltpu.SemaphoreType.DMA
    vmem = pltpu.VMEM
    scratch = [
        vmem((3, tok, width), BF),
        vmem((tok, width), BF),
        vmem((nz, 2, width, width), BF),
        vmem((3, 2 * nz * width, width), BF),
        vmem(near.shape, F32),
        vmem(far.shape, F32),
        vmem((nx, rows, HD), BF),
        vmem((nx, rows, HD), BF),
        vmem((ny, rows, HD), BF),
        vmem((nx, rows, HD), BF),
        vmem((nx, rows, HD), BF),
        vmem((tok, width), F32),
        vmem((2, tok, width), BF),
        vmem((nz, tok, width), F32),
        vmem((half_z, 2, tok // 2, width), BF),
        vmem((half_z, 2, tok // 2, width), BF),
        vmem((half_z, 2, tok // 2, width), BF),
        vmem((half_z, 2, tok // 2, width), BF),
        vmem((nz, 2, tok, width), BF),
        vmem((3, tok, width), F32),
        vmem((tok, HD), F32),
        vmem((2, tok, width), BF),
        vmem((2, tok, width), BF),
        dma((5,)),
        dma((nz,)),
        dma((nz,)),
        dma((nz,)),
        dma((nx,)),
        dma((nx,)),
        dma((ny,)),
        dma((ny,)),
        dma((nx,)),
        dma((nx,)),
        dma,
        dma,
        dma((half_z, 2)),
        dma((half_z, 2)),
        dma((half_z, 2)),
        dma((half_z, 2)),
        dma((half_z, 2)),
        dma((half_z, 2)),
        dma((half_z, 2)),
        dma((half_z, 2)),
        dma((nz, 2)),
        dma((nz, 2)),
        dma((2,)),
        dma((2,)),
    ]
    return pl.pallas_call(
        functools.partial(layer_pair, sizes, scale),
        name="layer_pair",
        out_shape=(jax.ShapeDtypeStruct((tok, width), BF),) * 2,
        in_specs=[anywhere] * 6,
        out_specs=(pl.BlockSpec(memory_space=pltpu.VMEM),) * 2,
        scratch_shapes=scratch,
        compiler_params=pltpu.CompilerParams(
            collective_id=0, has_side_effects=True, vmem_limit_bytes=48 * 1024 * 1024
        ),
    )(
        jnp.transpose(lin_qkv, (1, 0, 2)),
        resid,
        w_out,
        jnp.transpose(w_qkv, (1, 0, 2)),
        jnp.asarray(near),
        jnp.asarray(far),
    )


def on_torus(devices, sizes):
    finer = Mesh(devices.reshape(*sizes, 2), ("y", "x", "z", "c"))
    seq, head = ("y", "x"), ("z", "c")
    return jax.shard_map(
        functools.partial(local, sizes),
        mesh=finer,
        in_specs=(P(seq, None, head), P(seq, head), P(head, None), P(None, None, head)),
        out_specs=(P(seq, head), P(seq, head)),
        check_vma=False,
    )


def solution(mesh):
    side = math.isqrt(mesh.shape["seq"])
    return on_torus(mesh.devices, (side, side, mesh.shape["head"] // 2))
```

```python
import functools
import math

import jax
import jax.numpy as jnp
import numpy as np
from jax import lax
from jax.experimental import pallas as pl
from jax.experimental.pallas import tpu as pltpu
from jax.sharding import Mesh
from jax.sharding import PartitionSpec as P

HD = 128
BF = jnp.bfloat16
F32 = jnp.float32
MESH_ID = pl.DeviceIdType.MESH
PIECES = 4


def dot(a, b, contract=(1, 0)):
    dims = (((contract[0],), (contract[1],)), ((), ()))
    return lax.dot_general(a, b, dims, preferred_element_type=F32)


def remote(src, dst, send, recv, **where):
    return pltpu.make_async_remote_copy(
        src_ref=src, dst_ref=dst, send_sem=send, recv_sem=recv, device_id=where, device_id_type=MESH_ID
    )


def far_first(n):
    return sorted(range(1, n), key=lambda k: -min(k, n - k))


def layer_pair(
    sizes,
    scale,
    qkv_hbm,
    resid_hbm,
    wo_hbm,
    wq_hbm,
    near_hbm,
    far_hbm,
    hidden_ref,
    attended_ref,
    qkv,
    resid,
    w2,
    wq,
    near,
    far,
    st,
    p1,
    totals,
    p3s,
    p3,
    loc,
    lin2,
    part,
    out_r,
    in_r,
    out_l,
    in_l,
    hg,
    acc,
    sumsq,
    kv,
    kvp,
    qr,
    load_sem,
    wo_sem,
    wx_send,
    wx_recv,
    s1,
    r1,
    s2,
    r2,
    s3,
    r3,
    lin_send,
    lin_recv,
    rr_send,
    rr_recv,
    rl_send,
    rl_recv,
    gr_send,
    gr_recv,
    gl_send,
    gl_recv,
    gc_send,
    gc_recv,
    kv_send,
    kv_recv,
):
    ny, nx, nz = sizes
    half_z = nz // 2
    y, x, z, c = (lax.axis_index(name) for name in ("y", "x", "z", "c"))
    tok, width = resid.shape
    half = tok // 2
    halves = (pl.ds(0, half), pl.ds(half, half))
    rows_in = tok // PIECES
    piece_rows = [pl.ds(p * rows_in, rows_in) for p in range(PIECES)]
    early, late = list(range(PIECES // 2)), list(range(PIECES // 2, PIECES))
    heads = (pl.ds(0, HD), pl.ds(HD, HD))
    other = 1 - c
    right, left = lax.rem(z + 1, nz), lax.rem(z + nz - 1, nz)
    next_x = lax.rem(x + 1, nx)
    next_y = lax.rem(y + (x + 1) // nx, ny)
    prev_x = lax.rem(x + nx - 1, nx)
    prev_y = lax.rem(y + ny - 1 + (x + nx - 1) // nx, ny)
    block = y * nx + x

    sent = []

    def go(copy):
        copy.start()
        sent.append(copy)

    load_qkv = pltpu.make_async_copy(qkv_hbm, qkv, load_sem.at[0])
    load_qkv.start()
    barrier = pltpu.get_barrier_semaphore()
    greeted = 0
    places = [{"x": lax.rem(x + k, nx)} for k in range(1, nx)]
    places += [{"y": lax.rem(y + k, ny)} for k in range(1, ny)]
    places += [{"z": right}, {"z": left}, {"c": other}]
    places += [{"y": next_y, "x": next_x}, {"y": prev_y, "x": prev_x}]
    for place in places:
        pl.semaphore_signal(barrier, inc=1, device_id=place, device_id_type=MESH_ID)
        greeted += 1

    load_qkv.wait()
    for h in range(2):
        state = dot(qkv[1, :, heads[h]], qkv[2, :, heads[h]], (0, 0)).astype(BF)
        st[pl.ds(h * nx // 2, nx // 2)] = state.reshape(nx // 2, -1, HD)
    pl.semaphore_wait(barrier, greeted)

    def to_x(k):
        there = lax.rem(x + k, nx)
        return remote(st.at[there], p1.at[x], s1.at[k], r1.at[k], x=there)

    def from_x(k):
        there = lax.rem(x + nx - k, nx)
        return remote(st.at[there], p1.at[there], s1.at[k], r1.at[k], x=there)

    for k in far_first(nx):
        go(to_x(k))
    loads = [
        pltpu.make_async_copy(resid_hbm, resid, load_sem.at[1]),
        pltpu.make_async_copy(near_hbm, near, load_sem.at[2]),
        pltpu.make_async_copy(far_hbm, far, load_sem.at[3]),
        pltpu.make_async_copy(wq_hbm, wq, load_sem.at[4]),
    ]

    def wo_block(j, core):
        return wo_hbm.at[:, pl.ds(pl.multiple_of((2 * j + core) * width, width), width)]

    def wo_own(j):
        return pltpu.make_async_copy(wo_block(j, c), w2.at[j, c], wo_sem.at[j])

    def wo_swap(j, slot):
        return remote(wo_block(j, other), w2.at[j, slot], wx_send.at[j], wx_recv.at[j], c=other)

    for j in range(nz):
        wo_own(j).start()
        go(wo_swap(j, c))
    for load in loads:
        load.start()

    p1[pl.ds(x, 1)] = st[pl.ds(x, 1)]
    rows = lax.broadcasted_iota(jnp.int32, (tok, tok), 0)
    cols = lax.broadcasted_iota(jnp.int32, (tok, tok), 1)
    causal = cols <= rows
    for h in range(2):
        scores = dot(qkv[0, :, heads[h]], qkv[1, :, heads[h]], (1, 1))
        inner = jnp.where(causal, scores, 0.0).astype(BF)
        loc[:, heads[h]] = dot(inner, qkv[2, :, heads[h]])

    for k in far_first(nx)[::-1]:
        from_x(k).wait_recv()
    row_total = p1[0].astype(F32)
    for j in range(1, nx):
        row_total = row_total + p1[j].astype(F32)
    totals[pl.ds(y, 1)] = row_total.astype(BF)[None]

    def to_y(k):
        there = lax.rem(y + k, ny)
        return remote(totals.at[y], totals.at[y], s2.at[k], r2.at[k], y=there)

    def from_y(k):
        there = lax.rem(y + ny - k, ny)
        return remote(totals.at[there], totals.at[there], s2.at[k], r2.at[k], y=there)

    for k in far_first(ny):
        go(to_y(k))

    loads[1].wait()
    loads[2].wait()
    far_cos, far_sin = far[0, pl.ds(block, 1), :], far[1, pl.ds(block, 1), :]
    near_cos, near_sin = near[0], near[1]
    lane = lax.broadcasted_iota(jnp.int32, (tok, HD), 1)
    cosine = far_cos * near_cos - far_sin * near_sin
    sine = far_sin * near_cos + far_cos * near_sin
    near[0] = cosine
    near[1] = jnp.where(lane < HD // 2, -sine, sine)

    for k in far_first(ny)[::-1]:
        from_y(k).wait_recv()
    running = jnp.zeros_like(row_total)
    for j in range(ny):
        running = running + jnp.where(j < y, totals[j].astype(F32), 0.0)
    for j in range(nx):
        p3s[j] = running.astype(BF)
        running = running + p1[j].astype(F32)

    def back_x(k):
        there = lax.rem(x + k, nx)
        return remote(p3s.at[there], p3.at[x], s3.at[k], r3.at[k], x=there)

    def got_x(k):
        there = lax.rem(x + nx - k, nx)
        return remote(p3s.at[there], p3.at[there], s3.at[k], r3.at[k], x=there)

    for k in far_first(nx):
        go(back_x(k))
    p3[pl.ds(x, 1)] = p3s[pl.ds(x, 1)]
    for j in range(nz):
        wo_own(j).wait()
        wo_swap(j, other).wait_recv()
    loads[0].wait()
    for k in far_first(nx)[::-1]:
        got_x(k).wait_recv()

    for h in range(2):
        before = p3[pl.ds(h * nx // 2, nx // 2)].reshape(HD, HD)
        total = loc[:, heads[h]] + dot(qkv[0, :, heads[h]], before)
        lin2[c, :, heads[h]] = (total * scale).astype(BF)

    def lin_swap(slot):
        return remote(lin2.at[c], lin2.at[slot], lin_send, lin_recv, c=other)

    go(lin_swap(c))

    def own_part(j, _):
        part[j] = dot(lin2[c], w2[j, c])
        return 0

    lax.fori_loop(0, nz, own_part, 0)
    lin_swap(other).wait_recv()

    def at(k):
        return lax.rem(z + k + nz, nz)

    def finish_part(k):
        j = at(k)
        part[j] = part[j] + dot(lin2[other], w2[j, other])

    def ring_r(s, p):
        return remote(out_r.at[s, p], in_r.at[s, p], rr_send.at[s, p], rr_recv.at[s, p], z=right)

    def ring_l(s, p):
        return remote(out_l.at[s, p], in_l.at[s, p], rl_send.at[s, p], rl_recv.at[s, p], z=left)

    def pass_r(s, p, first=False):
        value = part[at(half_z - s), piece_rows[p]]
        if not first:
            ring_r(s - 1, p).wait_recv()
            value = value + in_r[s - 1, p].astype(F32)
        out_r[s, p] = value.astype(BF)
        go(ring_r(s, p))

    def pass_l(s, p, first=False):
        value = part[at(s - half_z), piece_rows[p]]
        if not first:
            ring_l(s - 1, p).wait_recv()
            value = value + in_l[s - 1, p].astype(F32)
        out_l[s, p] = value.astype(BF)
        go(ring_l(s, p))

    finish_part(half_z)
    for p, q in zip(early, late):
        pass_r(0, p, True)
        pass_l(0, q, True)
    finish_part(half_z - 1)
    for q in late:
        pass_r(1, q, True)
    finish_part(1 - half_z)
    for p in early:
        pass_l(1, p, True)
    for k in range(half_z - 2, 0, -1):
        finish_part(k)
        finish_part(-k)
    finish_part(0)
    for p, q in zip(early, late):
        pass_r(1, p)
        pass_l(1, q)
    for s in range(2, half_z):
        for p, q in zip(early, late):
            pass_r(s, q)
            pass_l(s, p)
        for p, q in zip(early, late):
            pass_r(s, p)
            pass_l(s, q)

    last = half_z - 1
    acc[...] = jnp.zeros_like(acc)
    sumsq[...] = jnp.zeros_like(sumsq)

    def piece(k, core, p):
        return hg.at[at(k), core, piece_rows[p]]

    def send_r(s, p):
        return remote(piece(-s, c, p), piece(-s, c, p), gr_send.at[s, p], gr_recv.at[s, p], z=right)

    def send_l(s, p):
        return remote(piece(s, c, p), piece(s, c, p), gl_send.at[s, p], gl_recv.at[s, p], z=left)

    def got_r(s, p):
        here = piece(-s - 1, c, p)
        remote(here, here, gr_send.at[s, p], gr_recv.at[s, p], z=right).wait_recv()

    def got_l(s, p):
        here = piece(s + 1, c, p)
        remote(here, here, gl_send.at[s, p], gl_recv.at[s, p], z=left).wait_recv()

    def core_copy(k, core, p):
        slot = lax.rem(k + nz, nz)
        here = piece(k, core, p)
        return remote(here, here, gc_send.at[slot, p], gc_recv.at[slot, p], c=other)

    for p in range(PIECES):
        if p in early:
            ring_l(last, p).wait_recv()
            ring_r(last, p).wait_recv()
        else:
            ring_r(last, p).wait_recv()
            ring_l(last, p).wait_recv()
        mixed = resid[piece_rows[p], :].astype(F32) + part[z, piece_rows[p]]
        mixed = mixed + in_r[last, p].astype(F32) + in_l[last, p].astype(F32)
        mixed = mixed.astype(BF)
        hg[z, c, piece_rows[p]] = mixed
        go(send_r(0, p))
        go(send_l(0, p))
        go(core_copy(0, c, p))
        hidden_ref[piece_rows[p], :] = mixed
    loads[3].wait()

    def project(k, core, h):
        j = at(k)
        values = hg[j, core, halves[h]]
        rows_of = pl.ds(pl.multiple_of((2 * j + core) * width, width), width)
        for i in range(3):
            acc[i, halves[h]] += dot(values, wq[i, rows_of, :])
        wide = values.astype(F32)
        squares = wide * wide
        sumsq[halves[h]] += squares[:, :HD] + squares[:, HD:]

    def project_other(k, h):
        for p in (early, late)[h]:
            core_copy(k, other, p).wait_recv()
        project(k, other, h)

    project(0, c, 0)
    project(0, c, 1)

    def gather_step(s, _):
        for h in range(2):
            for p in (early, late)[h]:
                got_r(s, p)
                if h == 0:
                    send_r(s + 1, p).start()
                else:
                    pl.when(s < last - 1)(lambda p=p: send_r(s + 1, p).start())
                core_copy(-1 - s, c, p).start()
                got_l(s, p)
                if h == 1:
                    send_l(s + 1, p).start()
                else:
                    pl.when(s < last - 1)(lambda p=p: send_l(s + 1, p).start())
                core_copy(s + 1, c, p).start()
            project(-1 - s, c, h)
            project(s + 1, c, h)
            project_other(-s, h)
            pl.when(s > 0)(lambda h=h: project_other(s, h))
        return 0

    lax.fori_loop(0, last, gather_step, 0)
    for s in range(1, half_z):
        sent += [send_r(s, p) for p in early]
        sent += [send_l(s, q) for q in late]
        if s < last:
            sent += [send_r(s, q) for q in late]
            sent += [send_l(s, p) for p in early]
    for k in range(1, nz):
        sent += [core_copy(k, c, p) for p in range(PIECES) if k != half_z]

    def kv_copy(h, i):
        return remote(kv.at[h, i], kvp.at[h, i], kv_send.at[h, i], kv_recv.at[h, i], y=next_y, x=next_x)

    def row_scale(h):
        mean = jnp.sum(sumsq[halves[h]], axis=1, keepdims=True) / (width * 2 * nz)
        return lax.rsqrt(mean + 1e-05)

    def rotated(i, h, head, scaled):
        values = acc[i, halves[h], heads[head]] * scaled
        return (values * near[0, halves[h]] + pltpu.roll(values, HD // 2, 1) * near[1, halves[h]]).astype(BF)

    for h in range(2):
        for p in (early, late)[h]:
            if h == 0:
                got_r(last, p)
            else:
                got_l(last, p)
            go(core_copy(half_z, c, p))
        project(half_z, c, h)
        project_other(-last, h)
        project_other(last, h)
        project_other(half_z, h)
        scaled = row_scale(h)
        for head in range(2):
            kv[h, 0, :, heads[head]] = rotated(1, h, head, scaled)
        go(kv_copy(h, 0))
        kv[h, 1] = (acc[2, halves[h]] * scaled).astype(BF)
        go(kv_copy(h, 1))
        for head in range(2):
            qr[halves[h], heads[head]] = rotated(0, h, head, scaled)

    score_scale = 1.0 / math.sqrt(HD)
    tops, sums, outs = [], [], []
    for head in range(2):
        q = qr[:, heads[head]]
        logits = []
        for h in range(2):
            value = dot(q, kv[h, 0, :, heads[head]], (1, 1)) * score_scale
            logits.append(jnp.where(causal[:, h * half : (h + 1) * half], value, -1e30))
        top = jnp.maximum(*(jnp.max(value, axis=1, keepdims=True) for value in logits))
        expos = [jnp.exp(value - top) for value in logits]
        tops.append(top)
        sums.append(sum(jnp.sum(expo, axis=1, keepdims=True) for expo in expos))
        outs.append(sum(dot(expos[h].astype(BF), kv[h, 1, :, heads[head]]) for h in range(2)))
    for h in range(2):
        kv_copy(h, 0).wait_recv()
        weights = []
        for head in range(2):
            logits = dot(qr[:, heads[head]], kvp[h, 0, :, heads[head]], (1, 1)) * score_scale
            logits = jnp.where(block > 0, logits, -1e30)
            top = jnp.maximum(tops[head], jnp.max(logits, axis=1, keepdims=True))
            expo = jnp.exp(logits - top)
            old = jnp.exp(tops[head] - top)
            tops[head] = top
            sums[head] = sums[head] * old + jnp.sum(expo, axis=1, keepdims=True)
            outs[head] = outs[head] * old
            weights.append(expo.astype(BF))
        kv_copy(h, 1).wait_recv()
        for head in range(2):
            outs[head] = outs[head] + dot(weights[head], kvp[h, 1, :, heads[head]])
    for head in range(2):
        attended_ref[:, heads[head]] = (outs[head] / sums[head]).astype(BF)

    for copy in sent:
        copy.wait_send()


def tables(tok, blocks):
    freq = 500000.0 ** (-(np.arange(HD // 2) * 2.0 / HD))
    freq = np.concatenate([freq, freq])
    near = np.arange(tok)[:, None] * freq
    far = (np.arange(blocks) * tok)[:, None] * freq
    return tuple(np.stack([np.cos(a), np.sin(a)]).astype(np.float32) for a in (near, far))


def local(sizes, lin_qkv, resid, w_out, w_qkv):
    ny, nx, nz = sizes
    tok, width = resid.shape
    half_z = nz // 2
    near, far = tables(tok, ny * nx)
    scale = 1.0 / math.sqrt(HD * tok * ny * nx)
    rows = 2 * HD // nx
    anywhere = pl.BlockSpec(memory_space=pltpu.HBM)
    dma = pltpu.SemaphoreType.DMA
    vmem = pltpu.VMEM
    scratch = [
        vmem((3, tok, width), BF),
        vmem((tok, width), BF),
        vmem((nz, 2, width, width), BF),
        vmem((3, 2 * nz * width, width), BF),
        vmem(near.shape, F32),
        vmem(far.shape, F32),
        vmem((nx, rows, HD), BF),
        vmem((nx, rows, HD), BF),
        vmem((ny, rows, HD), BF),
        vmem((nx, rows, HD), BF),
        vmem((nx, rows, HD), BF),
        vmem((tok, width), F32),
        vmem((2, tok, width), BF),
        vmem((nz, tok, width), F32),
        vmem((half_z, PIECES, tok // PIECES, width), BF),
        vmem((half_z, PIECES, tok // PIECES, width), BF),
        vmem((half_z, PIECES, tok // PIECES, width), BF),
        vmem((half_z, PIECES, tok // PIECES, width), BF),
        vmem((nz, 2, tok, width), BF),
        vmem((3, tok, width), F32),
        vmem((tok, HD), F32),
        vmem((2, 2, tok // 2, width), BF),
        vmem((2, 2, tok // 2, width), BF),
        vmem((tok, width), BF),
        dma((5,)),
        dma((nz,)),
        dma((nz,)),
        dma((nz,)),
        dma((nx,)),
        dma((nx,)),
        dma((ny,)),
        dma((ny,)),
        dma((nx,)),
        dma((nx,)),
        dma,
        dma,
        dma((half_z, PIECES)),
        dma((half_z, PIECES)),
        dma((half_z, PIECES)),
        dma((half_z, PIECES)),
        dma((half_z, PIECES)),
        dma((half_z, PIECES)),
        dma((half_z, PIECES)),
        dma((half_z, PIECES)),
        dma((nz, PIECES)),
        dma((nz, PIECES)),
        dma((2, 2)),
        dma((2, 2)),
    ]
    operands = (
        jnp.transpose(lin_qkv, (1, 0, 2)),
        resid,
        w_out,
        jnp.transpose(w_qkv, (1, 0, 2)),
        jnp.asarray(near),
        jnp.asarray(far),
    )
    return pl.pallas_call(
        functools.partial(layer_pair, sizes, scale),
        name="layer_pair",
        out_shape=(jax.ShapeDtypeStruct((tok, width), BF),) * 2,
        in_specs=[anywhere] * 6,
        out_specs=(pl.BlockSpec(memory_space=pltpu.VMEM),) * 2,
        scratch_shapes=scratch,
        compiler_params=pltpu.CompilerParams(
            collective_id=0, has_side_effects=True, vmem_limit_bytes=48 * 1024 * 1024
        ),
    )(
        *(pltpu.with_memory_space_constraint(array, pltpu.HBM) for array in operands)
    )


def on_torus(devices, sizes):
    finer = Mesh(devices.reshape(*sizes, 2), ("y", "x", "z", "c"))
    seq, head = ("y", "x"), ("z", "c")
    return jax.shard_map(
        functools.partial(local, sizes),
        mesh=finer,
        in_specs=(P(seq, None, head), P(seq, head), P(head, None), P(None, None, head)),
        out_specs=(P(seq, head), P(seq, head)),
        check_vma=False,
    )


def solution(mesh):
    side = math.isqrt(mesh.shape["seq"])
    return on_torus(mesh.devices, (side, side, mesh.shape["head"] // 2))
```

```python
import functools
import math

import jax
import jax.numpy as jnp
import numpy as np
from jax import lax
from jax.experimental import pallas as pl
from jax.experimental.pallas import tpu as pltpu
from jax.sharding import Mesh
from jax.sharding import PartitionSpec as P

HD = 128
BF = jnp.bfloat16
F32 = jnp.float32
MESH_ID = pl.DeviceIdType.MESH
PIECES = 4


def dot(a, b, contract=(1, 0)):
    dims = (((contract[0],), (contract[1],)), ((), ()))
    return lax.dot_general(a, b, dims, preferred_element_type=F32)


def remote(src, dst, send, recv, **where):
    return pltpu.make_async_remote_copy(
        src_ref=src, dst_ref=dst, send_sem=send, recv_sem=recv, device_id=where, device_id_type=MESH_ID
    )


def far_first(n):
    return sorted(range(1, n), key=lambda k: -min(k, n - k))


def layer_pair(
    sizes,
    scale,
    qkv_hbm,
    resid_hbm,
    wo_hbm,
    wq_hbm,
    near_hbm,
    far_hbm,
    hidden_ref,
    attended_ref,
    qkv,
    resid,
    w2,
    wq,
    near,
    far,
    st,
    p1,
    totals,
    p3s,
    p3,
    loc,
    lin2,
    part,
    out_r,
    in_r,
    out_l,
    in_l,
    far_out,
    far_in,
    hg,
    acc,
    sumsq,
    kv,
    kvp,
    qr,
    load_sem,
    wo_sem,
    wx_send,
    wx_recv,
    s1,
    r1,
    s2,
    r2,
    s3,
    r3,
    lin_send,
    lin_recv,
    rr_send,
    rr_recv,
    rl_send,
    rl_recv,
    rf_send,
    rf_recv,
    gr_send,
    gr_recv,
    gl_send,
    gl_recv,
    gc_send,
    gc_recv,
    kv_send,
    kv_recv,
):
    ny, nx, nz = sizes
    half_z = nz // 2
    y, x, z, c = (lax.axis_index(name) for name in ("y", "x", "z", "c"))
    tok, width = resid.shape
    half = tok // 2
    halves = (pl.ds(0, half), pl.ds(half, half))
    rows_in = tok // PIECES
    piece_rows = [pl.ds(p * rows_in, rows_in) for p in range(PIECES)]
    early, late = list(range(PIECES // 2)), list(range(PIECES // 2, PIECES))
    heads = (pl.ds(0, HD), pl.ds(HD, HD))
    other = 1 - c
    right, left = lax.rem(z + 1, nz), lax.rem(z + nz - 1, nz)
    next_x = lax.rem(x + 1, nx)
    next_y = lax.rem(y + (x + 1) // nx, ny)
    prev_x = lax.rem(x + nx - 1, nx)
    prev_y = lax.rem(y + ny - 1 + (x + nx - 1) // nx, ny)
    block = y * nx + x

    sent = []

    def go(copy):
        copy.start()
        sent.append(copy)

    load_qkv = pltpu.make_async_copy(qkv_hbm, qkv, load_sem.at[0])
    load_qkv.start()
    barrier = pltpu.get_barrier_semaphore()
    greeted = 0
    places = [{"x": lax.rem(x + k, nx)} for k in range(1, nx)]
    places += [{"y": lax.rem(y + k, ny)} for k in range(1, ny)]
    places += [{"z": right}, {"z": left}, {"z": lax.rem(z + 2, nz)}, {"z": lax.rem(z + nz - 2, nz)}, {"c": other}]
    places += [{"y": next_y, "x": next_x}, {"y": prev_y, "x": prev_x}]
    for place in places:
        pl.semaphore_signal(barrier, inc=1, device_id=place, device_id_type=MESH_ID)
        greeted += 1

    load_qkv.wait()
    for h in range(2):
        state = dot(qkv[1, :, heads[h]], qkv[2, :, heads[h]], (0, 0)).astype(BF)
        st[pl.ds(h * nx // 2, nx // 2)] = state.reshape(nx // 2, -1, HD)
    pl.semaphore_wait(barrier, greeted)

    def to_x(k):
        there = lax.rem(x + k, nx)
        return remote(st.at[there], p1.at[x], s1.at[k], r1.at[k], x=there)

    def from_x(k):
        there = lax.rem(x + nx - k, nx)
        return remote(st.at[there], p1.at[there], s1.at[k], r1.at[k], x=there)

    for k in far_first(nx):
        go(to_x(k))
    loads = [
        pltpu.make_async_copy(resid_hbm, resid, load_sem.at[1]),
        pltpu.make_async_copy(near_hbm, near, load_sem.at[2]),
        pltpu.make_async_copy(far_hbm, far, load_sem.at[3]),
        pltpu.make_async_copy(wq_hbm, wq, load_sem.at[4]),
    ]

    def wo_block(j, core):
        return wo_hbm.at[:, pl.ds(pl.multiple_of((2 * j + core) * width, width), width)]

    def wo_own(j):
        return pltpu.make_async_copy(wo_block(j, c), w2.at[j, c], wo_sem.at[j])

    def wo_swap(j, slot):
        return remote(wo_block(j, other), w2.at[j, slot], wx_send.at[j], wx_recv.at[j], c=other)

    for j in range(nz):
        wo_own(j).start()
        go(wo_swap(j, c))
    for load in loads:
        load.start()

    p1[pl.ds(x, 1)] = st[pl.ds(x, 1)]
    rows = lax.broadcasted_iota(jnp.int32, (tok, tok), 0)
    cols = lax.broadcasted_iota(jnp.int32, (tok, tok), 1)
    causal = cols <= rows
    for h in range(2):
        scores = dot(qkv[0, :, heads[h]], qkv[1, :, heads[h]], (1, 1))
        inner = jnp.where(causal, scores, 0.0).astype(BF)
        loc[:, heads[h]] = dot(inner, qkv[2, :, heads[h]])

    for k in far_first(nx)[::-1]:
        from_x(k).wait_recv()
    row_total = p1[0].astype(F32)
    for j in range(1, nx):
        row_total = row_total + p1[j].astype(F32)
    totals[pl.ds(y, 1)] = row_total.astype(BF)[None]

    def to_y(k):
        there = lax.rem(y + k, ny)
        return remote(totals.at[y], totals.at[y], s2.at[k], r2.at[k], y=there)

    def from_y(k):
        there = lax.rem(y + ny - k, ny)
        return remote(totals.at[there], totals.at[there], s2.at[k], r2.at[k], y=there)

    for k in range(ny - 1, 0, -1):
        pl.when(y < ny - k)(lambda k=k: to_y(k).start())

    loads[1].wait()
    loads[2].wait()
    far_cos, far_sin = far[0, pl.ds(block, 1), :], far[1, pl.ds(block, 1), :]
    near_cos, near_sin = near[0], near[1]
    lane = lax.broadcasted_iota(jnp.int32, (tok, HD), 1)
    cosine = far_cos * near_cos - far_sin * near_sin
    sine = far_sin * near_cos + far_cos * near_sin
    near[0] = cosine
    near[1] = jnp.where(lane < HD // 2, -sine, sine)

    for k in range(1, ny):
        pl.when(y >= k)(lambda k=k: from_y(k).wait_recv())
    running = jnp.zeros_like(row_total)
    for j in range(ny):
        running = running + jnp.where(j < y, totals[j].astype(F32), 0.0)
    for j in range(nx):
        p3s[j] = running.astype(BF)
        running = running + p1[j].astype(F32)

    def back_x(k):
        there = lax.rem(x + k, nx)
        return remote(p3s.at[there], p3.at[x], s3.at[k], r3.at[k], x=there)

    def got_x(k):
        there = lax.rem(x + nx - k, nx)
        return remote(p3s.at[there], p3.at[there], s3.at[k], r3.at[k], x=there)

    for k in far_first(nx):
        go(back_x(k))
    p3[pl.ds(x, 1)] = p3s[pl.ds(x, 1)]
    for j in range(nz):
        wo_own(j).wait()
        wo_swap(j, other).wait_recv()
    loads[0].wait()
    for k in far_first(nx)[::-1]:
        got_x(k).wait_recv()

    for h in range(2):
        before = p3[pl.ds(h * nx // 2, nx // 2)].reshape(HD, HD)
        total = loc[:, heads[h]] + dot(qkv[0, :, heads[h]], before)
        lin2[c, :, heads[h]] = (total * scale).astype(BF)

    def lin_swap(slot):
        return remote(lin2.at[c], lin2.at[slot], lin_send, lin_recv, c=other)

    go(lin_swap(c))

    def own_part(j, _):
        part[j] = dot(lin2[c], w2[j, c])
        return 0

    lax.fori_loop(0, nz, own_part, 0)
    lin_swap(other).wait_recv()

    def at(k):
        return lax.rem(z + k + nz, nz)

    def finish_part(k):
        j = at(k)
        part[j] = part[j] + dot(lin2[other], w2[j, other])

    def ring_r(s, p):
        return remote(out_r.at[s, p], in_r.at[s, p], rr_send.at[s, p], rr_recv.at[s, p], z=right)

    def ring_l(s, p):
        return remote(out_l.at[s, p], in_l.at[s, p], rl_send.at[s, p], rl_recv.at[s, p], z=left)

    def far_r(p):
        return remote(far_out.at[p], far_in.at[p], rf_send.at[p], rf_recv.at[p], z=at(2))

    def far_l(p):
        return remote(far_out.at[p], far_in.at[p], rf_send.at[p], rf_recv.at[p], z=at(-2))

    def pass_far(p):
        far_out[p] = part[at(half_z), piece_rows[p]].astype(BF)
        go(far_r(p) if p in early else far_l(p))

    def pass_r(s, p):
        value = part[at(half_z - s), piece_rows[p]]
        if s > 1:
            ring_r(s - 1, p).wait_recv()
            value = value + in_r[s - 1, p].astype(F32)
        if s == half_z - 2 and p in early:
            far_r(p).wait_recv()
            value = value + far_in[p].astype(F32)
        out_r[s, p] = value.astype(BF)
        go(ring_r(s, p))

    def pass_l(s, p):
        value = part[at(s - half_z), piece_rows[p]]
        if s > 1:
            ring_l(s - 1, p).wait_recv()
            value = value + in_l[s - 1, p].astype(F32)
        if s == half_z - 2 and p in late:
            far_l(p).wait_recv()
            value = value + far_in[p].astype(F32)
        out_l[s, p] = value.astype(BF)
        go(ring_l(s, p))

    finish_part(half_z)
    for p, q in zip(early, late):
        pass_far(p)
        pass_far(q)
    finish_part(half_z - 1)
    finish_part(1 - half_z)
    for p, q in zip(early, late):
        pass_r(1, p)
        pass_l(1, q)
    for p, q in zip(early, late):
        pass_r(1, q)
        pass_l(1, p)
    for k in range(half_z - 2, 0, -1):
        finish_part(k)
        finish_part(-k)
    finish_part(0)
    for s in range(2, half_z):
        for p, q in zip(early, late):
            pass_r(s, p)
            pass_l(s, q)
        for p, q in zip(early, late):
            pass_r(s, q)
            pass_l(s, p)

    last = half_z - 1
    acc[...] = jnp.zeros_like(acc)
    sumsq[...] = jnp.zeros_like(sumsq)

    def piece(k, core, p):
        return hg.at[at(k), core, piece_rows[p]]

    def send_r(s, p):
        return remote(piece(-s, c, p), piece(-s, c, p), gr_send.at[s, p], gr_recv.at[s, p], z=right)

    def send_l(s, p):
        return remote(piece(s, c, p), piece(s, c, p), gl_send.at[s, p], gl_recv.at[s, p], z=left)

    def jump_r(p):
        return remote(piece(0, c, p), piece(0, c, p), gr_send.at[1, p], gr_recv.at[1, p], z=at(2))

    def jump_l(p):
        return remote(piece(0, c, p), piece(0, c, p), gl_send.at[1, p], gl_recv.at[1, p], z=at(-2))

    def got_r(s, p):
        here = piece(-s - 1, c, p)
        remote(here, here, gr_send.at[s, p], gr_recv.at[s, p], z=right).wait_recv()

    def got_l(s, p):
        here = piece(s + 1, c, p)
        remote(here, here, gl_send.at[s, p], gl_recv.at[s, p], z=left).wait_recv()

    def core_copy(k, core, p):
        slot = lax.rem(k + nz, nz)
        here = piece(k, core, p)
        return remote(here, here, gc_send.at[slot, p], gc_recv.at[slot, p], c=other)

    for p in range(PIECES):
        if p in early:
            ring_l(last, p).wait_recv()
            ring_r(last, p).wait_recv()
        else:
            ring_r(last, p).wait_recv()
            ring_l(last, p).wait_recv()
        mixed = resid[piece_rows[p], :].astype(F32) + part[z, piece_rows[p]]
        mixed = mixed + in_r[last, p].astype(F32) + in_l[last, p].astype(F32)
        mixed = mixed.astype(BF)
        hg[z, c, piece_rows[p]] = mixed
        go(jump_r(p) if p in early else jump_l(p))
        go(send_r(0, p))
        go(send_l(0, p))
        go(core_copy(0, c, p))
        hidden_ref[piece_rows[p], :] = mixed
    loads[3].wait()

    def project(k, core, h):
        j = at(k)
        values = hg[j, core, halves[h]]
        rows_of = pl.ds(pl.multiple_of((2 * j + core) * width, width), width)
        for i in range(3):
            acc[i, halves[h]] += dot(values, wq[i, rows_of, :])
        wide = values.astype(F32)
        squares = wide * wide
        sumsq[halves[h]] += squares[:, :HD] + squares[:, HD:]

    def project_other(k, h):
        for p in (early, late)[h]:
            core_copy(k, other, p).wait_recv()
        project(k, other, h)

    project(0, c, 0)
    project(0, c, 1)

    def gather_step(s, _):
        for h in range(2):
            for p in (early, late)[h]:
                got_r(s, p)
                if h == 0:
                    pl.when(s > 0)(lambda p=p: send_r(s + 1, p).start())
                else:
                    pl.when(s < last - 1)(lambda p=p: send_r(s + 1, p).start())
                core_copy(-1 - s, c, p).start()
                got_l(s, p)
                if h == 1:
                    pl.when(s > 0)(lambda p=p: send_l(s + 1, p).start())
                else:
                    pl.when(s < last - 1)(lambda p=p: send_l(s + 1, p).start())
                core_copy(s + 1, c, p).start()
            project(-1 - s, c, h)
            project(s + 1, c, h)
            project_other(-s, h)
            pl.when(s > 0)(lambda h=h: project_other(s, h))
        return 0

    lax.fori_loop(0, last, gather_step, 0)
    for s in range(1, half_z):
        if s > 1:
            sent += [send_r(s, p) for p in early]
            sent += [send_l(s, q) for q in late]
        if s < last:
            sent += [send_r(s, q) for q in late]
            sent += [send_l(s, p) for p in early]
    for k in range(1, nz):
        sent += [core_copy(k, c, p) for p in range(PIECES) if k != half_z]

    def kv_copy(h, i):
        return remote(kv.at[h, i], kvp.at[h, i], kv_send.at[h, i], kv_recv.at[h, i], y=next_y, x=next_x)

    def row_scale(h):
        mean = jnp.sum(sumsq[halves[h]], axis=1, keepdims=True) / (width * 2 * nz)
        return lax.rsqrt(mean + 1e-05)

    def rotated(i, h, head, scaled):
        values = acc[i, halves[h], heads[head]] * scaled
        return (values * near[0, halves[h]] + pltpu.roll(values, HD // 2, 1) * near[1, halves[h]]).astype(BF)

    for h in range(2):
        for p in (early, late)[h]:
            if h == 0:
                got_r(last, p)
            else:
                got_l(last, p)
            go(core_copy(half_z, c, p))
        project(half_z, c, h)
        project_other(-last, h)
        project_other(last, h)
        project_other(half_z, h)
        scaled = row_scale(h)
        for head in range(2):
            kv[h, 0, :, heads[head]] = rotated(1, h, head, scaled)
        go(kv_copy(h, 0))
        kv[h, 1] = (acc[2, halves[h]] * scaled).astype(BF)
        go(kv_copy(h, 1))
        for head in range(2):
            qr[halves[h], heads[head]] = rotated(0, h, head, scaled)

    score_scale = 1.0 / math.sqrt(HD)
    tops, sums, outs = [], [], []
    for head in range(2):
        q = qr[:, heads[head]]
        logits = []
        for h in range(2):
            value = dot(q, kv[h, 0, :, heads[head]], (1, 1)) * score_scale
            logits.append(jnp.where(causal[:, h * half : (h + 1) * half], value, -1e30))
        top = jnp.maximum(*(jnp.max(value, axis=1, keepdims=True) for value in logits))
        expos = [jnp.exp(value - top) for value in logits]
        tops.append(top)
        sums.append(sum(jnp.sum(expo, axis=1, keepdims=True) for expo in expos))
        outs.append(sum(dot(expos[h].astype(BF), kv[h, 1, :, heads[head]]) for h in range(2)))
    for h in range(2):
        kv_copy(h, 0).wait_recv()
        weights = []
        for head in range(2):
            logits = dot(qr[:, heads[head]], kvp[h, 0, :, heads[head]], (1, 1)) * score_scale
            logits = jnp.where(block > 0, logits, -1e30)
            top = jnp.maximum(tops[head], jnp.max(logits, axis=1, keepdims=True))
            expo = jnp.exp(logits - top)
            old = jnp.exp(tops[head] - top)
            tops[head] = top
            sums[head] = sums[head] * old + jnp.sum(expo, axis=1, keepdims=True)
            outs[head] = outs[head] * old
            weights.append(expo.astype(BF))
        kv_copy(h, 1).wait_recv()
        for head in range(2):
            outs[head] = outs[head] + dot(weights[head], kvp[h, 1, :, heads[head]])
    for head in range(2):
        attended_ref[:, heads[head]] = (outs[head] / sums[head]).astype(BF)

    for copy in sent:
        copy.wait_send()
    for k in range(1, ny):
        pl.when(y < ny - k)(lambda k=k: to_y(k).wait_send())


def tables(tok, blocks):
    freq = 500000.0 ** (-(np.arange(HD // 2) * 2.0 / HD))
    freq = np.concatenate([freq, freq])
    near = np.arange(tok)[:, None] * freq
    far = (np.arange(blocks) * tok)[:, None] * freq
    return tuple(np.stack([np.cos(a), np.sin(a)]).astype(np.float32) for a in (near, far))


def local(sizes, lin_qkv, resid, w_out, w_qkv):
    ny, nx, nz = sizes
    tok, width = resid.shape
    half_z = nz // 2
    near, far = tables(tok, ny * nx)
    scale = 1.0 / math.sqrt(HD * tok * ny * nx)
    rows = 2 * HD // nx
    anywhere = pl.BlockSpec(memory_space=pltpu.HBM)
    dma = pltpu.SemaphoreType.DMA
    vmem = pltpu.VMEM
    scratch = [
        vmem((3, tok, width), BF),
        vmem((tok, width), BF),
        vmem((nz, 2, width, width), BF),
        vmem((3, 2 * nz * width, width), BF),
        vmem(near.shape, F32),
        vmem(far.shape, F32),
        vmem((nx, rows, HD), BF),
        vmem((nx, rows, HD), BF),
        vmem((ny, rows, HD), BF),
        vmem((nx, rows, HD), BF),
        vmem((nx, rows, HD), BF),
        vmem((tok, width), F32),
        vmem((2, tok, width), BF),
        vmem((nz, tok, width), F32),
        vmem((half_z, PIECES, tok // PIECES, width), BF),
        vmem((half_z, PIECES, tok // PIECES, width), BF),
        vmem((half_z, PIECES, tok // PIECES, width), BF),
        vmem((half_z, PIECES, tok // PIECES, width), BF),
        vmem((PIECES, tok // PIECES, width), BF),
        vmem((PIECES, tok // PIECES, width), BF),
        vmem((nz, 2, tok, width), BF),
        vmem((3, tok, width), F32),
        vmem((tok, HD), F32),
        vmem((2, 2, tok // 2, width), BF),
        vmem((2, 2, tok // 2, width), BF),
        vmem((tok, width), BF),
        dma((5,)),
        dma((nz,)),
        dma((nz,)),
        dma((nz,)),
        dma((nx,)),
        dma((nx,)),
        dma((ny,)),
        dma((ny,)),
        dma((nx,)),
        dma((nx,)),
        dma,
        dma,
        dma((half_z, PIECES)),
        dma((half_z, PIECES)),
        dma((half_z, PIECES)),
        dma((half_z, PIECES)),
        dma((PIECES,)),
        dma((PIECES,)),
        dma((half_z, PIECES)),
        dma((half_z, PIECES)),
        dma((half_z, PIECES)),
        dma((half_z, PIECES)),
        dma((nz, PIECES)),
        dma((nz, PIECES)),
        dma((2, 2)),
        dma((2, 2)),
    ]
    operands = (
        jnp.transpose(lin_qkv, (1, 0, 2)),
        resid,
        w_out,
        jnp.transpose(w_qkv, (1, 0, 2)),
        jnp.asarray(near),
        jnp.asarray(far),
    )
    return pl.pallas_call(
        functools.partial(layer_pair, sizes, scale),
        name="layer_pair",
        out_shape=(jax.ShapeDtypeStruct((tok, width), BF),) * 2,
        in_specs=[anywhere] * 6,
        out_specs=(pl.BlockSpec(memory_space=pltpu.VMEM),) * 2,
        scratch_shapes=scratch,
        compiler_params=pltpu.CompilerParams(
            collective_id=0, has_side_effects=True, vmem_limit_bytes=48 * 1024 * 1024
        ),
    )(
        *(pltpu.with_memory_space_constraint(array, pltpu.HBM) for array in operands)
    )


def on_torus(devices, sizes):
    finer = Mesh(devices.reshape(*sizes, 2), ("y", "x", "z", "c"))
    seq, head = ("y", "x"), ("z", "c")
    return jax.shard_map(
        functools.partial(local, sizes),
        mesh=finer,
        in_specs=(P(seq, None, head), P(seq, head), P(head, None), P(None, None, head)),
        out_specs=(P(seq, head), P(seq, head)),
        check_vma=False,
    )


def solution(mesh):
    side = math.isqrt(mesh.shape["seq"])
    return on_torus(mesh.devices, (side, side, mesh.shape["head"] // 2))
```

```python
import functools
import math

import jax
import jax.numpy as jnp
import numpy as np
from jax import lax
from jax.experimental import pallas as pl
from jax.experimental.pallas import tpu as pltpu
from jax.sharding import Mesh
from jax.sharding import PartitionSpec as P

HD = 128
BF = jnp.bfloat16
F32 = jnp.float32
MESH_ID = pl.DeviceIdType.MESH
PIECES = 4


def dot(a, b, contract=(1, 0)):
    dims = (((contract[0],), (contract[1],)), ((), ()))
    return lax.dot_general(a, b, dims, preferred_element_type=F32)


def remote(src, dst, send, recv, **where):
    return pltpu.make_async_remote_copy(
        src_ref=src, dst_ref=dst, send_sem=send, recv_sem=recv, device_id=where, device_id_type=MESH_ID
    )


def far_first(n):
    return sorted(range(1, n), key=lambda k: -min(k, n - k))


def layer_pair(
    sizes,
    scale,
    qkv_hbm,
    resid_hbm,
    wo_hbm,
    wq_hbm,
    near_hbm,
    far_hbm,
    out_ref,
    qkv,
    resid,
    w2,
    wq,
    near,
    far,
    st,
    p1,
    totals,
    p3s,
    p3,
    loc,
    lin2,
    part,
    out_r,
    in_r,
    out_l,
    in_l,
    far_out,
    far_in,
    hg,
    acc,
    sumsq,
    kv,
    kvp,
    qr,
    load_sem,
    wo_sem,
    wx_send,
    wx_recv,
    s1,
    r1,
    s2,
    r2,
    s3,
    r3,
    lin_send,
    lin_recv,
    rr_send,
    rr_recv,
    rl_send,
    rl_recv,
    rf_send,
    rf_recv,
    gr_send,
    gr_recv,
    gl_send,
    gl_recv,
    gc_send,
    gc_recv,
    kv_send,
    kv_recv,
):
    ny, nx, nz = sizes
    half_z = nz // 2
    y, x, z, c = (lax.axis_index(name) for name in ("y", "x", "z", "c"))
    tok, width = resid.shape
    half = tok // 2
    halves = (pl.ds(0, half), pl.ds(half, half))
    rows_in = tok // PIECES
    piece_rows = [pl.ds(p * rows_in, rows_in) for p in range(PIECES)]
    early, late = list(range(PIECES // 2)), list(range(PIECES // 2, PIECES))
    heads = (pl.ds(0, HD), pl.ds(HD, HD))
    other = 1 - c
    right, left = lax.rem(z + 1, nz), lax.rem(z + nz - 1, nz)
    next_x = lax.rem(x + 1, nx)
    next_y = lax.rem(y + (x + 1) // nx, ny)
    prev_x = lax.rem(x + nx - 1, nx)
    prev_y = lax.rem(y + ny - 1 + (x + nx - 1) // nx, ny)
    block = y * nx + x

    sent = []

    def go(copy):
        copy.start()
        sent.append(copy)

    load_qkv = pltpu.make_async_copy(qkv_hbm, qkv, load_sem.at[0])
    load_qkv.start()
    barrier = pltpu.get_barrier_semaphore()
    greeted = 0
    places = [{"x": lax.rem(x + k, nx)} for k in range(1, nx)]
    places += [{"y": lax.rem(y + k, ny)} for k in range(1, ny)]
    places += [{"z": right}, {"z": left}, {"z": lax.rem(z + 2, nz)}, {"z": lax.rem(z + nz - 2, nz)}, {"c": other}]
    places += [{"y": next_y, "x": next_x}, {"y": prev_y, "x": prev_x}]
    for place in places:
        pl.semaphore_signal(barrier, inc=1, device_id=place, device_id_type=MESH_ID)
        greeted += 1

    load_qkv.wait()
    for h in range(2):
        state = dot(qkv[1, :, heads[h]], qkv[2, :, heads[h]], (0, 0)).astype(BF)
        st[pl.ds(h * nx // 2, nx // 2)] = state.reshape(nx // 2, -1, HD)
    pl.semaphore_wait(barrier, greeted)

    def to_x(k):
        there = lax.rem(x + k, nx)
        return remote(st.at[there], p1.at[x], s1.at[k], r1.at[k], x=there)

    def from_x(k):
        there = lax.rem(x + nx - k, nx)
        return remote(st.at[there], p1.at[there], s1.at[k], r1.at[k], x=there)

    for k in far_first(nx):
        go(to_x(k))
    loads = [
        pltpu.make_async_copy(resid_hbm, resid, load_sem.at[1]),
        pltpu.make_async_copy(near_hbm, near, load_sem.at[2]),
        pltpu.make_async_copy(far_hbm, far, load_sem.at[3]),
        pltpu.make_async_copy(wq_hbm, wq, load_sem.at[4]),
    ]

    def wo_block(j, core):
        return wo_hbm.at[:, pl.ds(pl.multiple_of((2 * j + core) * width, width), width)]

    def wo_own(j):
        return pltpu.make_async_copy(wo_block(j, c), w2.at[j, c], wo_sem.at[j])

    def wo_swap(j, slot):
        return remote(wo_block(j, other), w2.at[j, slot], wx_send.at[j], wx_recv.at[j], c=other)

    for j in range(nz):
        wo_own(j).start()
        go(wo_swap(j, c))
    for load in loads:
        load.start()

    p1[pl.ds(x, 1)] = st[pl.ds(x, 1)]
    rows = lax.broadcasted_iota(jnp.int32, (tok, tok), 0)
    cols = lax.broadcasted_iota(jnp.int32, (tok, tok), 1)
    causal = cols <= rows
    for h in range(2):
        scores = dot(qkv[0, :, heads[h]], qkv[1, :, heads[h]], (1, 1))
        inner = jnp.where(causal, scores, 0.0).astype(BF)
        loc[:, heads[h]] = dot(inner, qkv[2, :, heads[h]])

    for k in far_first(nx)[::-1]:
        from_x(k).wait_recv()
    row_total = p1[0].astype(F32)
    for j in range(1, nx):
        row_total = row_total + p1[j].astype(F32)
    totals[pl.ds(y, 1)] = row_total.astype(BF)[None]

    def to_y(k):
        there = lax.rem(y + k, ny)
        return remote(totals.at[y], totals.at[y], s2.at[k], r2.at[k], y=there)

    def from_y(k):
        there = lax.rem(y + ny - k, ny)
        return remote(totals.at[there], totals.at[there], s2.at[k], r2.at[k], y=there)

    for k in range(ny - 1, 0, -1):
        pl.when(y < ny - k)(lambda k=k: to_y(k).start())

    loads[1].wait()
    loads[2].wait()
    far_cos, far_sin = far[0, pl.ds(block, 1), :], far[1, pl.ds(block, 1), :]
    near_cos, near_sin = near[0], near[1]
    lane = lax.broadcasted_iota(jnp.int32, (tok, HD), 1)
    cosine = far_cos * near_cos - far_sin * near_sin
    sine = far_sin * near_cos + far_cos * near_sin
    near[0] = cosine
    near[1] = jnp.where(lane < HD // 2, -sine, sine)

    for k in range(1, ny):
        pl.when(y >= k)(lambda k=k: from_y(k).wait_recv())
    running = jnp.zeros_like(row_total)
    for j in range(ny):
        running = running + jnp.where(j < y, totals[j].astype(F32), 0.0)
    for j in range(nx):
        p3s[j] = running.astype(BF)
        running = running + p1[j].astype(F32)

    def back_x(k):
        there = lax.rem(x + k, nx)
        return remote(p3s.at[there], p3.at[x], s3.at[k], r3.at[k], x=there)

    def got_x(k):
        there = lax.rem(x + nx - k, nx)
        return remote(p3s.at[there], p3.at[there], s3.at[k], r3.at[k], x=there)

    for k in far_first(nx):
        go(back_x(k))
    p3[pl.ds(x, 1)] = p3s[pl.ds(x, 1)]
    for j in range(nz):
        wo_own(j).wait()
        wo_swap(j, other).wait_recv()
    loads[0].wait()
    for k in far_first(nx)[::-1]:
        got_x(k).wait_recv()

    for h in range(2):
        before = p3[pl.ds(h * nx // 2, nx // 2)].reshape(HD, HD)
        total = loc[:, heads[h]] + dot(qkv[0, :, heads[h]], before)
        lin2[c, :, heads[h]] = (total * scale).astype(BF)

    def lin_swap(slot):
        return remote(lin2.at[c], lin2.at[slot], lin_send, lin_recv, c=other)

    go(lin_swap(c))

    def own_part(j, _):
        part[j] = dot(lin2[c], w2[j, c])
        return 0

    lax.fori_loop(0, nz, own_part, 0)
    lin_swap(other).wait_recv()

    def at(k):
        return lax.rem(z + k + nz, nz)

    def finish_part(k):
        j = at(k)
        part[j] = part[j] + dot(lin2[other], w2[j, other])

    def ring_r(s, p):
        return remote(out_r.at[s, p], in_r.at[s, p], rr_send.at[s, p], rr_recv.at[s, p], z=right)

    def ring_l(s, p):
        return remote(out_l.at[s, p], in_l.at[s, p], rl_send.at[s, p], rl_recv.at[s, p], z=left)

    def far_r(p):
        return remote(far_out.at[p], far_in.at[p], rf_send.at[p], rf_recv.at[p], z=at(2))

    def far_l(p):
        return remote(far_out.at[p], far_in.at[p], rf_send.at[p], rf_recv.at[p], z=at(-2))

    def pass_far(p):
        far_out[p] = part[at(half_z), piece_rows[p]].astype(BF)
        go(far_r(p) if p in early else far_l(p))

    def pass_r(s, p):
        value = part[at(half_z - s), piece_rows[p]]
        if s > 1:
            ring_r(s - 1, p).wait_recv()
            value = value + in_r[s - 1, p].astype(F32)
        if s == half_z - 2 and p in early:
            far_r(p).wait_recv()
            value = value + far_in[p].astype(F32)
        out_r[s, p] = value.astype(BF)
        go(ring_r(s, p))

    def pass_l(s, p):
        value = part[at(s - half_z), piece_rows[p]]
        if s > 1:
            ring_l(s - 1, p).wait_recv()
            value = value + in_l[s - 1, p].astype(F32)
        if s == half_z - 2 and p in late:
            far_l(p).wait_recv()
            value = value + far_in[p].astype(F32)
        out_l[s, p] = value.astype(BF)
        go(ring_l(s, p))

    finish_part(half_z)
    for p, q in zip(early, late):
        pass_far(p)
        pass_far(q)
    finish_part(half_z - 1)
    finish_part(1 - half_z)
    for p, q in zip(early, late):
        pass_r(1, p)
        pass_l(1, q)
    for p, q in zip(early, late):
        pass_r(1, q)
        pass_l(1, p)
    for k in range(half_z - 2, 0, -1):
        finish_part(k)
        finish_part(-k)
    finish_part(0)
    for s in range(2, half_z):
        for p, q in zip(early, late):
            pass_r(s, p)
            pass_l(s, q)
        for p, q in zip(early, late):
            pass_r(s, q)
            pass_l(s, p)

    last = half_z - 1
    acc[...] = jnp.zeros_like(acc)
    sumsq[...] = jnp.zeros_like(sumsq)

    def piece(k, core, p):
        return hg.at[at(k), core, piece_rows[p]]

    def send_r(s, p):
        return remote(piece(-s, c, p), piece(-s, c, p), gr_send.at[s, p], gr_recv.at[s, p], z=right)

    def send_l(s, p):
        return remote(piece(s, c, p), piece(s, c, p), gl_send.at[s, p], gl_recv.at[s, p], z=left)

    def jump_r(p):
        return remote(piece(0, c, p), piece(0, c, p), gr_send.at[1, p], gr_recv.at[1, p], z=at(2))

    def jump_l(p):
        return remote(piece(0, c, p), piece(0, c, p), gl_send.at[1, p], gl_recv.at[1, p], z=at(-2))

    def got_r(s, p):
        here = piece(-s - 1, c, p)
        remote(here, here, gr_send.at[s, p], gr_recv.at[s, p], z=right).wait_recv()

    def got_l(s, p):
        here = piece(s + 1, c, p)
        remote(here, here, gl_send.at[s, p], gl_recv.at[s, p], z=left).wait_recv()

    def core_copy(k, core, p):
        slot = lax.rem(k + nz, nz)
        here = piece(k, core, p)
        return remote(here, here, gc_send.at[slot, p], gc_recv.at[slot, p], c=other)

    for p in range(PIECES):
        ring_r(last, p).wait_recv()
        ring_l(last, p).wait_recv()
        mixed = resid[piece_rows[p], :].astype(F32) + part[z, piece_rows[p]]
        mixed = mixed + in_r[last, p].astype(F32) + in_l[last, p].astype(F32)
        mixed = mixed.astype(BF)
        hg[z, c, piece_rows[p]] = mixed
        go(jump_r(p) if p in early else send_r(0, p))
        go(send_l(0, p) if p in early else jump_l(p))
        go(core_copy(0, c, p))
        out_ref[0, piece_rows[p], :] = mixed
    for p, q in zip(early, late):
        go(send_r(0, p))
        go(send_l(0, q))
    loads[3].wait()

    def project(k, core, rows):
        j = at(k)
        values = hg[j, core, rows]
        rows_of = pl.ds(pl.multiple_of((2 * j + core) * width, width), width)
        for i in range(3):
            acc[i, rows] += dot(values, wq[i, rows_of, :])
        wide = values.astype(F32)
        squares = wide * wide
        sumsq[rows] += squares[:, :HD] + squares[:, HD:]

    def project_pair(k, core, rows):
        def one(i, _):
            project(k * (1 - 2 * i), core, rows)
            return 0

        lax.fori_loop(0, 2, one, 0)

    def from_core(k, pieces):
        for p in pieces:
            core_copy(k, other, p).wait_recv()

    def take_r(s, pieces, forward):
        for p in pieces:
            got_r(s, p)
            if forward:
                go(send_r(s + 1, p))
            go(core_copy(-1 - s, c, p))

    def take_l(s, pieces, forward):
        for p in pieces:
            got_l(s, p)
            if forward:
                go(send_l(s + 1, p))
            go(core_copy(s + 1, c, p))

    every, whole = early + late, pl.ds(0, tok)
    project(0, c, whole)
    take_r(1, early, True)
    take_l(0, early, True)
    take_r(0, late, True)
    take_l(1, late, True)
    take_r(0, early, False)
    take_l(0, late, False)
    from_core(0, every)
    project(0, other, whole)
    project_pair(1, c, whole)
    for s in range(2, last):
        take_r(s, early, True)
        take_l(s - 1, early, True)
        take_r(s - 1, late, True)
        take_l(s, late, True)
        from_core(1 - s, every)
        from_core(s - 1, every)
        project_pair(s, c, whole)
        project_pair(s - 1, other, whole)

    def kv_copy(h, i):
        return remote(kv.at[h, i], kvp.at[h, i], kv_send.at[h, i], kv_recv.at[h, i], y=next_y, x=next_x)

    def row_scale(h):
        mean = jnp.sum(sumsq[halves[h]], axis=1, keepdims=True) / (width * 2 * nz)
        return lax.rsqrt(mean + 1e-05)

    def rotated(i, h, head, scaled):
        values = acc[i, halves[h], heads[head]] * scaled
        return (values * near[0, halves[h]] + pltpu.roll(values, HD // 2, 1) * near[1, halves[h]]).astype(BF)

    take_r(last, early, False)
    take_l(last - 1, early, False)
    project_pair(last, c, halves[0])
    project(half_z, c, halves[0])
    from_core(1 - last, every)
    from_core(last - 1, every)
    project_pair(last - 1, other, whole)
    take_r(last - 1, late, False)
    take_l(last, late, False)
    for h in range(2):
        pieces = (early, late)[h]
        if h == 1:
            project_pair(last, c, halves[1])
            project(half_z, c, halves[1])
        from_core(-last, pieces)
        from_core(last, pieces)
        from_core(half_z, pieces)
        project_pair(last, other, halves[h])
        project(half_z, other, halves[h])
        scaled = row_scale(h)
        for head in range(2):
            kv[h, 0, :, heads[head]] = rotated(1, h, head, scaled)
        go(kv_copy(h, 0))
        kv[h, 1] = (acc[2, halves[h]] * scaled).astype(BF)
        go(kv_copy(h, 1))
        for head in range(2):
            qr[halves[h], heads[head]] = rotated(0, h, head, scaled)

    score_scale = 1.0 / math.sqrt(HD)
    tops, sums, outs = [], [], []
    for head in range(2):
        q = qr[:, heads[head]]
        logits = []
        for h in range(2):
            value = dot(q, kv[h, 0, :, heads[head]], (1, 1)) * score_scale
            logits.append(jnp.where(causal[:, h * half : (h + 1) * half], value, -1e30))
        top = jnp.maximum(*(jnp.max(value, axis=1, keepdims=True) for value in logits))
        expos = [jnp.exp(value - top) for value in logits]
        tops.append(top)
        sums.append(sum(jnp.sum(expo, axis=1, keepdims=True) for expo in expos))
        outs.append(sum(dot(expos[h].astype(BF), kv[h, 1, :, heads[head]]) for h in range(2)))
    for h in range(2):
        kv_copy(h, 0).wait_recv()
        weights = []
        for head in range(2):
            logits = dot(qr[:, heads[head]], kvp[h, 0, :, heads[head]], (1, 1)) * score_scale
            logits = jnp.where(block > 0, logits, -1e30)
            top = jnp.maximum(tops[head], jnp.max(logits, axis=1, keepdims=True))
            expo = jnp.exp(logits - top)
            old = jnp.exp(tops[head] - top)
            tops[head] = top
            sums[head] = sums[head] * old + jnp.sum(expo, axis=1, keepdims=True)
            outs[head] = outs[head] * old
            weights.append(expo.astype(BF))
        kv_copy(h, 1).wait_recv()
        for head in range(2):
            outs[head] = outs[head] + dot(weights[head], kvp[h, 1, :, heads[head]])
    for head in range(2):
        out_ref[1, :, heads[head]] = (outs[head] / sums[head]).astype(BF)

    for copy in sent:
        copy.wait_send()
    for k in range(1, ny):
        pl.when(y < ny - k)(lambda k=k: to_y(k).wait_send())


def tables(tok, blocks):
    freq = 500000.0 ** (-(np.arange(HD // 2) * 2.0 / HD))
    freq = np.concatenate([freq, freq])
    near = np.arange(tok)[:, None] * freq
    far = (np.arange(blocks) * tok)[:, None] * freq
    return tuple(np.stack([np.cos(a), np.sin(a)]).astype(np.float32) for a in (near, far))


def local(sizes, lin_qkv, resid, w_out, w_qkv):
    ny, nx, nz = sizes
    tok, width = resid.shape
    half_z = nz // 2
    near, far = tables(tok, ny * nx)
    scale = 1.0 / math.sqrt(HD * tok * ny * nx)
    rows = 2 * HD // nx
    anywhere = pl.BlockSpec(memory_space=pltpu.HBM)
    dma = pltpu.SemaphoreType.DMA
    vmem = pltpu.VMEM
    scratch = [
        vmem((3, tok, width), BF),
        vmem((tok, width), BF),
        vmem((nz, 2, width, width), BF),
        vmem((3, 2 * nz * width, width), BF),
        vmem(near.shape, F32),
        vmem(far.shape, F32),
        vmem((nx, rows, HD), BF),
        vmem((nx, rows, HD), BF),
        vmem((ny, rows, HD), BF),
        vmem((nx, rows, HD), BF),
        vmem((nx, rows, HD), BF),
        vmem((tok, width), F32),
        vmem((2, tok, width), BF),
        vmem((nz, tok, width), F32),
        vmem((half_z, PIECES, tok // PIECES, width), BF),
        vmem((half_z, PIECES, tok // PIECES, width), BF),
        vmem((half_z, PIECES, tok // PIECES, width), BF),
        vmem((half_z, PIECES, tok // PIECES, width), BF),
        vmem((PIECES, tok // PIECES, width), BF),
        vmem((PIECES, tok // PIECES, width), BF),
        vmem((nz, 2, tok, width), BF),
        vmem((3, tok, width), F32),
        vmem((tok, HD), F32),
        vmem((2, 2, tok // 2, width), BF),
        vmem((2, 2, tok // 2, width), BF),
        vmem((tok, width), BF),
        dma((5,)),
        dma((nz,)),
        dma((nz,)),
        dma((nz,)),
        dma((nx,)),
        dma((nx,)),
        dma((ny,)),
        dma((ny,)),
        dma((nx,)),
        dma((nx,)),
        dma,
        dma,
        dma((half_z, PIECES)),
        dma((half_z, PIECES)),
        dma((half_z, PIECES)),
        dma((half_z, PIECES)),
        dma((PIECES,)),
        dma((PIECES,)),
        dma((half_z, PIECES)),
        dma((half_z, PIECES)),
        dma((half_z, PIECES)),
        dma((half_z, PIECES)),
        dma((nz, PIECES)),
        dma((nz, PIECES)),
        dma((2, 2)),
        dma((2, 2)),
    ]
    operands = (
        jnp.transpose(lin_qkv, (1, 0, 2)),
        resid,
        w_out,
        jnp.transpose(w_qkv, (1, 0, 2)),
        jnp.asarray(near),
        jnp.asarray(far),
    )
    both = pl.pallas_call(
        functools.partial(layer_pair, sizes, scale),
        name="layer_pair",
        out_shape=jax.ShapeDtypeStruct((2, tok, width), BF),
        in_specs=[anywhere] * 6,
        out_specs=pl.BlockSpec(memory_space=pltpu.VMEM),
        scratch_shapes=scratch,
        compiler_params=pltpu.CompilerParams(
            collective_id=0, has_side_effects=True, vmem_limit_bytes=48 * 1024 * 1024
        ),
    )(
        *(pltpu.with_memory_space_constraint(array, pltpu.HBM) for array in operands)
    )
    return both[0], both[1]


def on_torus(devices, sizes):
    finer = Mesh(devices.reshape(*sizes, 2), ("y", "x", "z", "c"))
    seq, head = ("y", "x"), ("z", "c")
    return jax.shard_map(
        functools.partial(local, sizes),
        mesh=finer,
        in_specs=(P(seq, None, head), P(seq, head), P(head, None), P(None, None, head)),
        out_specs=(P(seq, head), P(seq, head)),
        check_vma=False,
    )


def solution(mesh):
    side = math.isqrt(mesh.shape["seq"])
    return on_torus(mesh.devices, (side, side, mesh.shape["head"] // 2))
```

```python
import functools
import math

import jax
import jax.numpy as jnp
import numpy as np
from jax import lax
from jax.experimental import pallas as pl
from jax.experimental.pallas import tpu as pltpu
from jax.sharding import Mesh
from jax.sharding import PartitionSpec as P

HD = 128
BF = jnp.bfloat16
F32 = jnp.float32
MESH_ID = pl.DeviceIdType.MESH
PIECES = 4


def dot(a, b, contract=(1, 0)):
    dims = (((contract[0],), (contract[1],)), ((), ()))
    return lax.dot_general(a, b, dims, preferred_element_type=F32)


def remote(src, dst, send, recv, **where):
    return pltpu.make_async_remote_copy(
        src_ref=src, dst_ref=dst, send_sem=send, recv_sem=recv, device_id=where, device_id_type=MESH_ID
    )


def far_first(n):
    return sorted(range(1, n), key=lambda k: -min(k, n - k))


def layer_pair(
    sizes,
    scale,
    qkv_hbm,
    resid_hbm,
    wo_hbm,
    wq_hbm,
    near_hbm,
    far_hbm,
    out_ref,
    qkv,
    resid,
    w2,
    wq,
    near,
    far,
    st,
    p1,
    totals,
    p3s,
    p3,
    p3x,
    qx,
    locx,
    loc,
    lin2,
    part,
    out_r,
    in_r,
    out_l,
    in_l,
    far_out,
    far_in,
    hg,
    acc,
    sumsq,
    kv,
    kvp,
    qr,
    load_sem,
    wo_sem,
    wx_send,
    wx_recv,
    s1,
    r1,
    s2,
    r2,
    s3,
    r3,
    s4,
    r4,
    qx_send,
    qx_recv,
    lx_send,
    lx_recv,
    rr_send,
    rr_recv,
    rl_send,
    rl_recv,
    rf_send,
    rf_recv,
    gr_send,
    gr_recv,
    gl_send,
    gl_recv,
    gc_send,
    gc_recv,
    kv_send,
    kv_recv,
):
    ny, nx, nz = sizes
    half_z = nz // 2
    y, x, z, c = (lax.axis_index(name) for name in ("y", "x", "z", "c"))
    tok, width = resid.shape
    half = tok // 2
    halves = (pl.ds(0, half), pl.ds(half, half))
    rows_in = tok // PIECES
    piece_rows = [pl.ds(p * rows_in, rows_in) for p in range(PIECES)]
    early, late = list(range(PIECES // 2)), list(range(PIECES // 2, PIECES))
    heads = (pl.ds(0, HD), pl.ds(HD, HD))
    other = 1 - c
    right, left = lax.rem(z + 1, nz), lax.rem(z + nz - 1, nz)
    next_x = lax.rem(x + 1, nx)
    next_y = lax.rem(y + (x + 1) // nx, ny)
    prev_x = lax.rem(x + nx - 1, nx)
    prev_y = lax.rem(y + ny - 1 + (x + nx - 1) // nx, ny)
    block = y * nx + x

    sent = []

    def go(copy):
        copy.start()
        sent.append(copy)

    load_qkv = pltpu.make_async_copy(qkv_hbm, qkv, load_sem.at[0])
    load_qkv.start()
    barrier = pltpu.get_barrier_semaphore()
    greeted = 0
    places = [{"x": lax.rem(x + k, nx)} for k in range(1, nx)]
    places += [{"x": lax.rem(x + k, nx), "c": other} for k in range(1, nx)]
    places += [{"y": lax.rem(y + k, ny)} for k in range(1, ny)]
    places += [{"z": right}, {"z": left}, {"z": lax.rem(z + 2, nz)}, {"z": lax.rem(z + nz - 2, nz)}, {"c": other}]
    places += [{"y": next_y, "x": next_x}, {"y": prev_y, "x": prev_x}]
    for place in places:
        pl.semaphore_signal(barrier, inc=1, device_id=place, device_id_type=MESH_ID)
        greeted += 1

    load_qkv.wait()
    for h in range(2):
        state = dot(qkv[1, :, heads[h]], qkv[2, :, heads[h]], (0, 0)).astype(BF)
        st[pl.ds(h * nx // 2, nx // 2)] = state.reshape(nx // 2, -1, HD)
    pl.semaphore_wait(barrier, greeted)

    def to_x(k):
        there = lax.rem(x + k, nx)
        return remote(st.at[there], p1.at[x], s1.at[k], r1.at[k], x=there)

    def from_x(k):
        there = lax.rem(x + nx - k, nx)
        return remote(st.at[there], p1.at[there], s1.at[k], r1.at[k], x=there)

    for k in far_first(nx):
        go(to_x(k))
    loads = [
        pltpu.make_async_copy(resid_hbm, resid, load_sem.at[1]),
        pltpu.make_async_copy(near_hbm, near, load_sem.at[2]),
        pltpu.make_async_copy(far_hbm, far, load_sem.at[3]),
        pltpu.make_async_copy(wq_hbm, wq, load_sem.at[4]),
    ]

    def wo_block(j, core):
        return wo_hbm.at[:, pl.ds(pl.multiple_of((2 * j + core) * width, width), width)]

    def wo_own(j):
        return pltpu.make_async_copy(wo_block(j, c), w2.at[j, c], wo_sem.at[j])

    def wo_swap(j, slot):
        return remote(wo_block(j, other), w2.at[j, slot], wx_send.at[j], wx_recv.at[j], c=other)

    for j in range(nz):
        wo_own(j).start()
        go(wo_swap(j, c))
    for load in loads:
        load.start()

    def query_swap():
        return remote(qkv.at[0], qx, qx_send, qx_recv, c=other)

    def loc_swap():
        return remote(loc, locx, lx_send, lx_recv, c=other)

    go(query_swap())
    p1[pl.ds(x, 1)] = st[pl.ds(x, 1)]
    rows = lax.broadcasted_iota(jnp.int32, (tok, tok), 0)
    cols = lax.broadcasted_iota(jnp.int32, (tok, tok), 1)
    causal = cols <= rows
    for h in range(2):
        scores = dot(qkv[0, :, heads[h]], qkv[1, :, heads[h]], (1, 1))
        inner = jnp.where(causal, scores, 0.0).astype(BF)
        loc[:, heads[h]] = dot(inner, qkv[2, :, heads[h]])
    go(loc_swap())

    for k in far_first(nx)[::-1]:
        from_x(k).wait_recv()
    row_total = p1[0].astype(F32)
    for j in range(1, nx):
        row_total = row_total + p1[j].astype(F32)
    totals[pl.ds(y, 1)] = row_total.astype(BF)[None]

    def to_y(k):
        there = lax.rem(y + k, ny)
        return remote(totals.at[y], totals.at[y], s2.at[k], r2.at[k], y=there)

    def from_y(k):
        there = lax.rem(y + ny - k, ny)
        return remote(totals.at[there], totals.at[there], s2.at[k], r2.at[k], y=there)

    for k in range(ny - 1, 0, -1):
        pl.when(y < ny - k)(lambda k=k: to_y(k).start())

    loads[1].wait()
    loads[2].wait()
    far_cos, far_sin = far[0, pl.ds(block, 1), :], far[1, pl.ds(block, 1), :]
    near_cos, near_sin = near[0], near[1]
    lane = lax.broadcasted_iota(jnp.int32, (tok, HD), 1)
    cosine = far_cos * near_cos - far_sin * near_sin
    sine = far_sin * near_cos + far_cos * near_sin
    near[0] = cosine
    near[1] = jnp.where(lane < HD // 2, -sine, sine)

    for k in range(1, ny):
        pl.when(y >= k)(lambda k=k: from_y(k).wait_recv())
    running = jnp.zeros_like(row_total)
    for j in range(ny):
        running = running + jnp.where(j < y, totals[j].astype(F32), 0.0)
    for j in range(nx):
        p3s[j] = running.astype(BF)
        running = running + p1[j].astype(F32)

    def back_x(k):
        there = lax.rem(x + k, nx)
        return remote(p3s.at[there], p3.at[x], s3.at[k], r3.at[k], x=there)

    def got_x(k):
        there = lax.rem(x + nx - k, nx)
        return remote(p3s.at[there], p3.at[there], s3.at[k], r3.at[k], x=there)

    def cross_x(k):
        there = lax.rem(x + k, nx)
        return remote(p3s.at[there], p3x.at[x], s4.at[k], r4.at[k], x=there, c=other)

    def crossed_x(k):
        there = lax.rem(x + nx - k, nx)
        return remote(p3s.at[there], p3x.at[there], s4.at[k], r4.at[k], x=there, c=other)

    for k in far_first(nx):
        go(back_x(k))
        go(cross_x(k))
    go(cross_x(0))
    p3[pl.ds(x, 1)] = p3s[pl.ds(x, 1)]
    for j in range(nz):
        wo_own(j).wait()
        wo_swap(j, other).wait_recv()
    loads[0].wait()
    query_swap().wait_recv()
    loc_swap().wait_recv()
    crossed_x(0).wait_recv()
    for k in far_first(nx)[::-1]:
        got_x(k).wait_recv()
        crossed_x(k).wait_recv()

    for h in range(2):
        before = p3[pl.ds(h * nx // 2, nx // 2)].reshape(HD, HD)
        total = loc[:, heads[h]] + dot(qkv[0, :, heads[h]], before)
        lin2[c, :, heads[h]] = (total * scale).astype(BF)
        before = p3x[pl.ds(h * nx // 2, nx // 2)].reshape(HD, HD)
        total = locx[:, heads[h]] + dot(qx[:, heads[h]], before)
        lin2[other, :, heads[h]] = (total * scale).astype(BF)

    def at(k):
        return lax.rem(z + k + nz, nz)

    def finish_part(k):
        j = at(k)
        part[j] = dot(lin2[c], w2[j, c]) + dot(lin2[other], w2[j, other])

    def ring_r(s, p):
        return remote(out_r.at[s, p], in_r.at[s, p], rr_send.at[s, p], rr_recv.at[s, p], z=right)

    def ring_l(s, p):
        return remote(out_l.at[s, p], in_l.at[s, p], rl_send.at[s, p], rl_recv.at[s, p], z=left)

    def far_r(p):
        return remote(far_out.at[p], far_in.at[p], rf_send.at[p], rf_recv.at[p], z=at(2))

    def far_l(p):
        return remote(far_out.at[p], far_in.at[p], rf_send.at[p], rf_recv.at[p], z=at(-2))

    def pass_far(p):
        far_out[p] = part[at(half_z), piece_rows[p]].astype(BF)
        go(far_r(p) if p in early else far_l(p))

    def pass_r(s, p):
        value = part[at(half_z - s), piece_rows[p]]
        if s > 1:
            ring_r(s - 1, p).wait_recv()
            value = value + in_r[s - 1, p].astype(F32)
        if s == half_z - 2 and p in early:
            far_r(p).wait_recv()
            value = value + far_in[p].astype(F32)
        out_r[s, p] = value.astype(BF)
        go(ring_r(s, p))

    def pass_l(s, p):
        value = part[at(s - half_z), piece_rows[p]]
        if s > 1:
            ring_l(s - 1, p).wait_recv()
            value = value + in_l[s - 1, p].astype(F32)
        if s == half_z - 2 and p in late:
            far_l(p).wait_recv()
            value = value + far_in[p].astype(F32)
        out_l[s, p] = value.astype(BF)
        go(ring_l(s, p))

    finish_part(half_z)
    for p, q in zip(early, late):
        pass_far(p)
        pass_far(q)
    finish_part(half_z - 1)
    finish_part(1 - half_z)
    for p, q in zip(early, late):
        pass_r(1, p)
        pass_l(1, q)
    for p, q in zip(early, late):
        pass_r(1, q)
        pass_l(1, p)
    for k in range(half_z - 2, 0, -1):
        finish_part(k)
        finish_part(-k)
    finish_part(0)
    for s in range(2, half_z):
        for p, q in zip(early, late):
            pass_r(s, p)
            pass_l(s, q)
        for p, q in zip(early, late):
            pass_r(s, q)
            pass_l(s, p)

    last = half_z - 1
    acc[...] = jnp.zeros_like(acc)
    sumsq[...] = jnp.zeros_like(sumsq)

    def piece(k, core, p):
        return hg.at[at(k), core, piece_rows[p]]

    def send_r(s, p):
        return remote(piece(-s, c, p), piece(-s, c, p), gr_send.at[s, p], gr_recv.at[s, p], z=right)

    def send_l(s, p):
        return remote(piece(s, c, p), piece(s, c, p), gl_send.at[s, p], gl_recv.at[s, p], z=left)

    def jump_r(p):
        return remote(piece(0, c, p), piece(0, c, p), gr_send.at[1, p], gr_recv.at[1, p], z=at(2))

    def jump_l(p):
        return remote(piece(0, c, p), piece(0, c, p), gl_send.at[1, p], gl_recv.at[1, p], z=at(-2))

    def got_r(s, p):
        here = piece(-s - 1, c, p)
        remote(here, here, gr_send.at[s, p], gr_recv.at[s, p], z=right).wait_recv()

    def got_l(s, p):
        here = piece(s + 1, c, p)
        remote(here, here, gl_send.at[s, p], gl_recv.at[s, p], z=left).wait_recv()

    def core_copy(k, core, p):
        slot = lax.rem(k + nz, nz)
        here = piece(k, core, p)
        return remote(here, here, gc_send.at[slot, p], gc_recv.at[slot, p], c=other)

    for p in range(PIECES):
        ring_r(last, p).wait_recv()
        ring_l(last, p).wait_recv()
        mixed = resid[piece_rows[p], :].astype(F32) + part[z, piece_rows[p]]
        mixed = mixed + in_r[last, p].astype(F32) + in_l[last, p].astype(F32)
        mixed = mixed.astype(BF)
        hg[z, c, piece_rows[p]] = mixed
        go(jump_r(p) if p in early else send_r(0, p))
        go(send_l(0, p) if p in early else jump_l(p))
        go(core_copy(0, c, p))
        out_ref[0, piece_rows[p], :] = mixed
    for p, q in zip(early, late):
        go(send_r(0, p))
        go(send_l(0, q))
    loads[3].wait()

    def project(k, core, rows):
        j = at(k)
        values = hg[j, core, rows]
        rows_of = pl.ds(pl.multiple_of((2 * j + core) * width, width), width)
        for i in range(3):
            acc[i, rows] += dot(values, wq[i, rows_of, :])
        wide = values.astype(F32)
        squares = wide * wide
        sumsq[rows] += squares[:, :HD] + squares[:, HD:]

    def project_pair(k, core, rows):
        def one(i, _):
            project(k * (1 - 2 * i), core, rows)
            return 0

        lax.fori_loop(0, 2, one, 0)

    def from_core(k, pieces):
        for p in pieces:
            core_copy(k, other, p).wait_recv()

    def take_r(s, pieces, forward):
        for p in pieces:
            got_r(s, p)
            if forward:
                go(send_r(s + 1, p))
            go(core_copy(-1 - s, c, p))

    def take_l(s, pieces, forward):
        for p in pieces:
            got_l(s, p)
            if forward:
                go(send_l(s + 1, p))
            go(core_copy(s + 1, c, p))

    every, whole = early + late, pl.ds(0, tok)
    project(0, c, whole)
    take_r(1, early, True)
    take_l(0, early, True)
    take_r(0, late, True)
    take_l(1, late, True)
    take_r(0, early, False)
    take_l(0, late, False)
    from_core(0, every)
    project(0, other, whole)
    project_pair(1, c, whole)
    for s in range(2, last):
        take_r(s, early, True)
        take_l(s - 1, early, True)
        take_r(s - 1, late, True)
        take_l(s, late, True)
        from_core(1 - s, every)
        from_core(s - 1, every)
        project_pair(s, c, whole)
        project_pair(s - 1, other, whole)

    def kv_copy(h, i):
        return remote(kv.at[h, i], kvp.at[h, i], kv_send.at[h, i], kv_recv.at[h, i], y=next_y, x=next_x)

    def row_scale(h):
        mean = jnp.sum(sumsq[halves[h]], axis=1, keepdims=True) / (width * 2 * nz)
        return lax.rsqrt(mean + 1e-05)

    def rotated(i, h, head, scaled):
        values = acc[i, halves[h], heads[head]] * scaled
        return (values * near[0, halves[h]] + pltpu.roll(values, HD // 2, 1) * near[1, halves[h]]).astype(BF)

    take_r(last, early, False)
    take_l(last - 1, early, False)
    project_pair(last, c, halves[0])
    project(half_z, c, halves[0])
    from_core(1 - last, every)
    from_core(last - 1, every)
    project_pair(last - 1, other, whole)
    take_r(last - 1, late, False)
    take_l(last, late, False)
    for h in range(2):
        pieces = (early, late)[h]
        if h == 1:
            project_pair(last, c, halves[1])
            project(half_z, c, halves[1])
        from_core(-last, pieces)
        from_core(last, pieces)
        from_core(half_z, pieces)
        project_pair(last, other, halves[h])
        project(half_z, other, halves[h])
        scaled = row_scale(h)
        for head in range(2):
            kv[h, 0, :, heads[head]] = rotated(1, h, head, scaled)
        go(kv_copy(h, 0))
        kv[h, 1] = (acc[2, halves[h]] * scaled).astype(BF)
        go(kv_copy(h, 1))
        for head in range(2):
            qr[halves[h], heads[head]] = rotated(0, h, head, scaled)

    score_scale = 1.0 / math.sqrt(HD)
    tops, sums, outs = [], [], []
    for head in range(2):
        q = qr[:, heads[head]]
        logits = []
        for h in range(2):
            value = dot(q, kv[h, 0, :, heads[head]], (1, 1)) * score_scale
            logits.append(jnp.where(causal[:, h * half : (h + 1) * half], value, -1e30))
        top = jnp.maximum(*(jnp.max(value, axis=1, keepdims=True) for value in logits))
        expos = [jnp.exp(value - top) for value in logits]
        tops.append(top)
        sums.append(sum(jnp.sum(expo, axis=1, keepdims=True) for expo in expos))
        outs.append(sum(dot(expos[h].astype(BF), kv[h, 1, :, heads[head]]) for h in range(2)))
    for h in range(2):
        kv_copy(h, 0).wait_recv()
        weights = []
        for head in range(2):
            logits = dot(qr[:, heads[head]], kvp[h, 0, :, heads[head]], (1, 1)) * score_scale
            logits = jnp.where(block > 0, logits, -1e30)
            top = jnp.maximum(tops[head], jnp.max(logits, axis=1, keepdims=True))
            expo = jnp.exp(logits - top)
            old = jnp.exp(tops[head] - top)
            tops[head] = top
            sums[head] = sums[head] * old + jnp.sum(expo, axis=1, keepdims=True)
            outs[head] = outs[head] * old
            weights.append(expo.astype(BF))
        kv_copy(h, 1).wait_recv()
        for head in range(2):
            outs[head] = outs[head] + dot(weights[head], kvp[h, 1, :, heads[head]])
    for head in range(2):
        out_ref[1, :, heads[head]] = (outs[head] / sums[head]).astype(BF)

    for copy in sent:
        copy.wait_send()
    for k in range(1, ny):
        pl.when(y < ny - k)(lambda k=k: to_y(k).wait_send())


def tables(tok, blocks):
    freq = 500000.0 ** (-(np.arange(HD // 2) * 2.0 / HD))
    freq = np.concatenate([freq, freq])
    near = np.arange(tok)[:, None] * freq
    far = (np.arange(blocks) * tok)[:, None] * freq
    return tuple(np.stack([np.cos(a), np.sin(a)]).astype(np.float32) for a in (near, far))


def local(sizes, lin_qkv, resid, w_out, w_qkv):
    ny, nx, nz = sizes
    tok, width = resid.shape
    half_z = nz // 2
    near, far = tables(tok, ny * nx)
    scale = 1.0 / math.sqrt(HD * tok * ny * nx)
    rows = 2 * HD // nx
    anywhere = pl.BlockSpec(memory_space=pltpu.HBM)
    dma = pltpu.SemaphoreType.DMA
    vmem = pltpu.VMEM
    scratch = [
        vmem((3, tok, width), BF),
        vmem((tok, width), BF),
        vmem((nz, 2, width, width), BF),
        vmem((3, 2 * nz * width, width), BF),
        vmem(near.shape, F32),
        vmem(far.shape, F32),
        vmem((nx, rows, HD), BF),
        vmem((nx, rows, HD), BF),
        vmem((ny, rows, HD), BF),
        vmem((nx, rows, HD), BF),
        vmem((nx, rows, HD), BF),
        vmem((nx, rows, HD), BF),
        vmem((tok, width), BF),
        vmem((tok, width), F32),
        vmem((tok, width), F32),
        vmem((2, tok, width), BF),
        vmem((nz, tok, width), F32),
        vmem((half_z, PIECES, tok // PIECES, width), BF),
        vmem((half_z, PIECES, tok // PIECES, width), BF),
        vmem((half_z, PIECES, tok // PIECES, width), BF),
        vmem((half_z, PIECES, tok // PIECES, width), BF),
        vmem((PIECES, tok // PIECES, width), BF),
        vmem((PIECES, tok // PIECES, width), BF),
        vmem((nz, 2, tok, width), BF),
        vmem((3, tok, width), F32),
        vmem((tok, HD), F32),
        vmem((2, 2, tok // 2, width), BF),
        vmem((2, 2, tok // 2, width), BF),
        vmem((tok, width), BF),
        dma((5,)),
        dma((nz,)),
        dma((nz,)),
        dma((nz,)),
        dma((nx,)),
        dma((nx,)),
        dma((ny,)),
        dma((ny,)),
        dma((nx,)),
        dma((nx,)),
        dma((nx,)),
        dma((nx,)),
        dma,
        dma,
        dma,
        dma,
        dma((half_z, PIECES)),
        dma((half_z, PIECES)),
        dma((half_z, PIECES)),
        dma((half_z, PIECES)),
        dma((PIECES,)),
        dma((PIECES,)),
        dma((half_z, PIECES)),
        dma((half_z, PIECES)),
        dma((half_z, PIECES)),
        dma((half_z, PIECES)),
        dma((nz, PIECES)),
        dma((nz, PIECES)),
        dma((2, 2)),
        dma((2, 2)),
    ]
    operands = (
        jnp.transpose(lin_qkv, (1, 0, 2)),
        resid,
        w_out,
        jnp.transpose(w_qkv, (1, 0, 2)),
        jnp.asarray(near),
        jnp.asarray(far),
    )
    both = pl.pallas_call(
        functools.partial(layer_pair, sizes, scale),
        name="layer_pair",
        out_shape=jax.ShapeDtypeStruct((2, tok, width), BF),
        in_specs=[anywhere] * 6,
        out_specs=pl.BlockSpec(memory_space=pltpu.VMEM),
        scratch_shapes=scratch,
        compiler_params=pltpu.CompilerParams(
            collective_id=0, has_side_effects=True, vmem_limit_bytes=48 * 1024 * 1024
        ),
    )(
        *(pltpu.with_memory_space_constraint(array, pltpu.HBM) for array in operands)
    )
    return both[0], both[1]


def on_torus(devices, sizes):
    finer = Mesh(devices.reshape(*sizes, 2), ("y", "x", "z", "c"))
    seq, head = ("y", "x"), ("z", "c")
    return jax.shard_map(
        functools.partial(local, sizes),
        mesh=finer,
        in_specs=(P(seq, None, head), P(seq, head), P(head, None), P(None, None, head)),
        out_specs=(P(seq, head), P(seq, head)),
        check_vma=False,
    )


def solution(mesh):
    side = math.isqrt(mesh.shape["seq"])
    return on_torus(mesh.devices, (side, side, mesh.shape["head"] // 2))
```

```python
import functools
import math

import jax
import jax.numpy as jnp
import numpy as np
from jax import lax
from jax.experimental import pallas as pl
from jax.experimental.pallas import tpu as pltpu
from jax.sharding import Mesh
from jax.sharding import PartitionSpec as P

HD = 128
BF = jnp.bfloat16
F32 = jnp.float32
MESH_ID = pl.DeviceIdType.MESH
PIECES = 4


def dot(a, b, contract=(1, 0)):
    dims = (((contract[0],), (contract[1],)), ((), ()))
    return lax.dot_general(a, b, dims, preferred_element_type=F32)


def remote(src, dst, send, recv, **where):
    return pltpu.make_async_remote_copy(
        src_ref=src, dst_ref=dst, send_sem=send, recv_sem=recv, device_id=where, device_id_type=MESH_ID
    )


def far_first(n):
    return sorted(range(1, n), key=lambda k: -min(k, n - k))


def layer_pair(
    sizes,
    scale,
    qkv_hbm,
    resid_hbm,
    wo_hbm,
    wq_hbm,
    near_hbm,
    far_hbm,
    out_ref,
    qkv,
    resid,
    w2,
    wq,
    near,
    far,
    st,
    p1,
    totals,
    p3s,
    p3,
    p3x,
    qx,
    locx,
    loc,
    lin2,
    part,
    out_r,
    in_r,
    out_l,
    in_l,
    far_out,
    far_in,
    hg,
    acc,
    sumsq,
    kv,
    kvp,
    qr,
    load_sem,
    wo_sem,
    wx_send,
    wx_recv,
    s1,
    r1,
    s2,
    r2,
    s3,
    r3,
    s4,
    r4,
    qx_send,
    qx_recv,
    lx_send,
    lx_recv,
    rr_send,
    rr_recv,
    rl_send,
    rl_recv,
    rf_send,
    rf_recv,
    gr_send,
    gr_recv,
    gl_send,
    gl_recv,
    gc_send,
    gc_recv,
    kv_send,
    kv_recv,
):
    ny, nx, nz = sizes
    half_z = nz // 2
    y, x, z, c = (lax.axis_index(name) for name in ("y", "x", "z", "c"))
    tok, width = resid.shape
    half = tok // 2
    halves = (pl.ds(0, half), pl.ds(half, half))
    rows_in = tok // PIECES
    piece_rows = [pl.ds(p * rows_in, rows_in) for p in range(PIECES)]
    early, late = list(range(PIECES // 2)), list(range(PIECES // 2, PIECES))
    heads = (pl.ds(0, HD), pl.ds(HD, HD))
    other = 1 - c
    right, left = lax.rem(z + 1, nz), lax.rem(z + nz - 1, nz)
    next_x = lax.rem(x + 1, nx)
    next_y = lax.rem(y + (x + 1) // nx, ny)
    prev_x = lax.rem(x + nx - 1, nx)
    prev_y = lax.rem(y + ny - 1 + (x + nx - 1) // nx, ny)
    block = y * nx + x

    sent = []

    def go(copy):
        copy.start()
        sent.append(copy)

    load_qkv = pltpu.make_async_copy(qkv_hbm, qkv, load_sem.at[0])
    load_qkv.start()
    barrier = pltpu.get_barrier_semaphore()
    greeted = 0
    places = [{"x": lax.rem(x + k, nx)} for k in range(1, nx)]
    places += [{"x": lax.rem(x + k, nx), "c": other} for k in range(1, nx)]
    places += [{"y": lax.rem(y + k, ny)} for k in range(1, ny)]
    places += [{"z": right}, {"z": left}, {"z": lax.rem(z + 2, nz)}, {"z": lax.rem(z + nz - 2, nz)}, {"c": other}]
    places += [{"y": next_y, "x": next_x}, {"y": prev_y, "x": prev_x}]
    for place in places:
        pl.semaphore_signal(barrier, inc=1, device_id=place, device_id_type=MESH_ID)
        greeted += 1

    load_qkv.wait()
    for h in range(2):
        state = dot(qkv[1, :, heads[h]], qkv[2, :, heads[h]], (0, 0)).astype(BF)
        st[pl.ds(h * nx // 2, nx // 2)] = state.reshape(nx // 2, -1, HD)
    pl.semaphore_wait(barrier, greeted)

    def to_x(k):
        there = lax.rem(x + k, nx)
        return remote(st.at[there], p1.at[x], s1.at[k], r1.at[k], x=there)

    def from_x(k):
        there = lax.rem(x + nx - k, nx)
        return remote(st.at[there], p1.at[there], s1.at[k], r1.at[k], x=there)

    for k in far_first(nx):
        go(to_x(k))
    loads = [
        pltpu.make_async_copy(resid_hbm, resid, load_sem.at[1]),
        pltpu.make_async_copy(near_hbm, near, load_sem.at[2]),
        pltpu.make_async_copy(far_hbm, far, load_sem.at[3]),
        pltpu.make_async_copy(wq_hbm, wq, load_sem.at[4]),
    ]

    def wo_block(j, core):
        return wo_hbm.at[:, pl.ds(pl.multiple_of((2 * j + core) * width, width), width)]

    def wo_own(j):
        return pltpu.make_async_copy(wo_block(j, c), w2.at[j, c], wo_sem.at[j])

    def wo_swap(j, slot):
        return remote(wo_block(j, other), w2.at[j, slot], wx_send.at[j], wx_recv.at[j], c=other)

    for j in range(nz):
        wo_own(j).start()
        go(wo_swap(j, c))
    for load in loads:
        load.start()

    def query_swap():
        return remote(qkv.at[0], qx, qx_send, qx_recv, c=other)

    def loc_swap():
        return remote(loc, locx, lx_send, lx_recv, c=other)

    go(query_swap())
    p1[pl.ds(x, 1)] = st[pl.ds(x, 1)]
    rows = lax.broadcasted_iota(jnp.int32, (tok, tok), 0)
    cols = lax.broadcasted_iota(jnp.int32, (tok, tok), 1)
    causal = cols <= rows
    for h in range(2):
        scores = dot(qkv[0, :, heads[h]], qkv[1, :, heads[h]], (1, 1))
        inner = jnp.where(causal, scores, 0.0).astype(BF)
        loc[:, heads[h]] = dot(inner, qkv[2, :, heads[h]])
    go(loc_swap())

    for k in far_first(nx)[::-1]:
        from_x(k).wait_recv()
    row_total = p1[0].astype(F32)
    for j in range(1, nx):
        row_total = row_total + p1[j].astype(F32)
    totals[pl.ds(y, 1)] = row_total.astype(BF)[None]

    def to_y(k):
        there = lax.rem(y + k, ny)
        return remote(totals.at[y], totals.at[y], s2.at[k], r2.at[k], y=there)

    def from_y(k):
        there = lax.rem(y + ny - k, ny)
        return remote(totals.at[there], totals.at[there], s2.at[k], r2.at[k], y=there)

    for k in range(ny - 1, 0, -1):
        pl.when(y < ny - k)(lambda k=k: to_y(k).start())

    loads[1].wait()
    loads[2].wait()
    far_cos, far_sin = far[0, pl.ds(block, 1), :], far[1, pl.ds(block, 1), :]
    near_cos, near_sin = near[0], near[1]
    lane = lax.broadcasted_iota(jnp.int32, (tok, HD), 1)
    cosine = far_cos * near_cos - far_sin * near_sin
    sine = far_sin * near_cos + far_cos * near_sin
    near[0] = cosine
    near[1] = jnp.where(lane < HD // 2, -sine, sine)

    for k in range(1, ny):
        pl.when(y >= k)(lambda k=k: from_y(k).wait_recv())
    running = jnp.zeros_like(row_total)
    for j in range(ny):
        running = running + jnp.where(j < y, totals[j].astype(F32), 0.0)
    for j in range(nx):
        p3s[j] = running.astype(BF)
        running = running + p1[j].astype(F32)

    def back_x(k):
        there = lax.rem(x + k, nx)
        return remote(p3s.at[there], p3.at[x], s3.at[k], r3.at[k], x=there)

    def got_x(k):
        there = lax.rem(x + nx - k, nx)
        return remote(p3s.at[there], p3.at[there], s3.at[k], r3.at[k], x=there)

    def cross_x(k):
        there = lax.rem(x + k, nx)
        return remote(p3s.at[there], p3x.at[x], s4.at[k], r4.at[k], x=there, c=other)

    def crossed_x(k):
        there = lax.rem(x + nx - k, nx)
        return remote(p3s.at[there], p3x.at[there], s4.at[k], r4.at[k], x=there, c=other)

    for k in far_first(nx):
        go(back_x(k))
        go(cross_x(k))
    go(cross_x(0))
    p3[pl.ds(x, 1)] = p3s[pl.ds(x, 1)]
    for j in range(nz):
        wo_own(j).wait()
        wo_swap(j, other).wait_recv()
    loads[0].wait()
    query_swap().wait_recv()
    loc_swap().wait_recv()
    crossed_x(0).wait_recv()
    for k in far_first(nx)[::-1]:
        got_x(k).wait_recv()
        crossed_x(k).wait_recv()

    for h in range(2):
        before = p3[pl.ds(h * nx // 2, nx // 2)].reshape(HD, HD)
        total = loc[:, heads[h]] + dot(qkv[0, :, heads[h]], before)
        lin2[c, :, heads[h]] = (total * scale).astype(BF)
        before = p3x[pl.ds(h * nx // 2, nx // 2)].reshape(HD, HD)
        total = locx[:, heads[h]] + dot(qx[:, heads[h]], before)
        lin2[other, :, heads[h]] = (total * scale).astype(BF)

    def at(k):
        return lax.rem(z + k + nz, nz)

    def finish_part(k):
        j = at(k)
        part[j] = dot(lin2[c], w2[j, c]) + dot(lin2[other], w2[j, other])

    def ring_r(s, p):
        return remote(out_r.at[s, p], in_r.at[s, p], rr_send.at[s, p], rr_recv.at[s, p], z=right)

    def ring_l(s, p):
        return remote(out_l.at[s, p], in_l.at[s, p], rl_send.at[s, p], rl_recv.at[s, p], z=left)

    def far_r(p):
        return remote(far_out.at[p], far_in.at[p], rf_send.at[p], rf_recv.at[p], z=at(2))

    def far_l(p):
        return remote(far_out.at[p], far_in.at[p], rf_send.at[p], rf_recv.at[p], z=at(-2))

    def pass_far(p):
        far_out[p] = part[at(half_z), piece_rows[p]].astype(BF)
        go(far_r(p) if p in early else far_l(p))

    def pass_r(s, p):
        value = part[at(half_z - s), piece_rows[p]]
        if s > 1:
            ring_r(s - 1, p).wait_recv()
            value = value + in_r[s - 1, p].astype(F32)
        if s == half_z - 2 and p in early:
            far_r(p).wait_recv()
            value = value + far_in[p].astype(F32)
        out_r[s, p] = value.astype(BF)
        go(ring_r(s, p))

    def pass_l(s, p):
        value = part[at(s - half_z), piece_rows[p]]
        if s > 1:
            ring_l(s - 1, p).wait_recv()
            value = value + in_l[s - 1, p].astype(F32)
        if s == half_z - 2 and p in late:
            far_l(p).wait_recv()
            value = value + far_in[p].astype(F32)
        out_l[s, p] = value.astype(BF)
        go(ring_l(s, p))

    finish_part(half_z)
    for p, q in zip(early, late):
        pass_far(p)
        pass_far(q)
    finish_part(half_z - 1)
    finish_part(1 - half_z)
    for p, q in zip(early, late):
        pass_r(1, p)
        pass_l(1, q)
    for p, q in zip(early, late):
        pass_r(1, q)
        pass_l(1, p)
    for k in range(half_z - 2, 0, -1):
        finish_part(k)
        finish_part(-k)
    finish_part(0)
    for s in range(2, half_z):
        for p in early + late:
            pass_r(s, p)
            pass_l(s, p)

    last = half_z - 1
    acc[...] = jnp.zeros_like(acc)
    sumsq[...] = jnp.zeros_like(sumsq)

    def piece(k, core, p):
        return hg.at[at(k), core, piece_rows[p]]

    def send_r(s, p):
        return remote(piece(-s, c, p), piece(-s, c, p), gr_send.at[s, p], gr_recv.at[s, p], z=right)

    def send_l(s, p):
        return remote(piece(s, c, p), piece(s, c, p), gl_send.at[s, p], gl_recv.at[s, p], z=left)

    def jump_r(p):
        return remote(piece(0, c, p), piece(0, c, p), gr_send.at[1, p], gr_recv.at[1, p], z=at(2))

    def jump_l(p):
        return remote(piece(0, c, p), piece(0, c, p), gl_send.at[1, p], gl_recv.at[1, p], z=at(-2))

    def got_r(s, p):
        here = piece(-s - 1, c, p)
        remote(here, here, gr_send.at[s, p], gr_recv.at[s, p], z=right).wait_recv()

    def got_l(s, p):
        here = piece(s + 1, c, p)
        remote(here, here, gl_send.at[s, p], gl_recv.at[s, p], z=left).wait_recv()

    def core_copy(k, core, p):
        slot = lax.rem(k + nz, nz)
        here = piece(k, core, p)
        return remote(here, here, gc_send.at[slot, p], gc_recv.at[slot, p], c=other)

    for p in range(PIECES):
        ring_r(last, p).wait_recv()
        ring_l(last, p).wait_recv()
        mixed = resid[piece_rows[p], :].astype(F32) + part[z, piece_rows[p]]
        mixed = mixed + in_r[last, p].astype(F32) + in_l[last, p].astype(F32)
        mixed = mixed.astype(BF)
        hg[z, c, piece_rows[p]] = mixed
        go(jump_r(p) if p in early else send_r(0, p))
        go(send_l(0, p) if p in early else jump_l(p))
        go(core_copy(0, c, p))
        out_ref[0, piece_rows[p], :] = mixed
    for p, q in zip(early, late):
        go(send_r(0, p))
        go(send_l(0, q))
    loads[3].wait()

    def project(k, core, rows):
        j = at(k)
        values = hg[j, core, rows]
        rows_of = pl.ds(pl.multiple_of((2 * j + core) * width, width), width)
        for i in range(3):
            acc[i, rows] += dot(values, wq[i, rows_of, :])
        wide = values.astype(F32)
        squares = wide * wide
        sumsq[rows] += squares[:, :HD] + squares[:, HD:]

    def project_pair(k, core, rows):
        def one(i, _):
            project(k * (1 - 2 * i), core, rows)
            return 0

        lax.fori_loop(0, 2, one, 0)

    def from_core(k, pieces):
        for p in pieces:
            core_copy(k, other, p).wait_recv()

    def take_r(s, pieces, forward):
        for p in pieces:
            got_r(s, p)
            if forward:
                go(send_r(s + 1, p))
            go(core_copy(-1 - s, c, p))

    def take_l(s, pieces, forward):
        for p in pieces:
            got_l(s, p)
            if forward:
                go(send_l(s + 1, p))
            go(core_copy(s + 1, c, p))

    every, whole = early + late, pl.ds(0, tok)
    project(0, c, whole)
    take_r(1, early, True)
    take_l(0, early, True)
    take_r(0, late, True)
    take_l(1, late, True)
    take_r(0, early, False)
    take_l(0, late, False)
    from_core(0, every)
    project(0, other, whole)
    project_pair(1, c, whole)
    for s in range(2, last):
        take_r(s, early, True)
        take_l(s - 1, early, True)
        take_r(s - 1, late, True)
        take_l(s, late, True)
        from_core(1 - s, every)
        from_core(s - 1, every)
        project_pair(s, c, whole)
        project_pair(s - 1, other, whole)

    def kv_copy(h, i):
        return remote(kv.at[h, i], kvp.at[h, i], kv_send.at[h, i], kv_recv.at[h, i], y=next_y, x=next_x)

    def row_scale(h):
        mean = jnp.sum(sumsq[halves[h]], axis=1, keepdims=True) / (width * 2 * nz)
        return lax.rsqrt(mean + 1e-05)

    def rotated(i, h, head, scaled):
        values = acc[i, halves[h], heads[head]] * scaled
        return (values * near[0, halves[h]] + pltpu.roll(values, HD // 2, 1) * near[1, halves[h]]).astype(BF)

    take_r(last, early, False)
    take_l(last - 1, early, False)
    project_pair(last, c, halves[0])
    project(half_z, c, halves[0])
    from_core(1 - last, every)
    from_core(last - 1, every)
    project_pair(last - 1, other, whole)
    take_r(last - 1, late, False)
    take_l(last, late, False)
    for h in range(2):
        pieces = (early, late)[h]
        if h == 1:
            project_pair(last, c, halves[1])
            project(half_z, c, halves[1])
        from_core(-last, pieces)
        from_core(last, pieces)
        from_core(half_z, pieces)
        project_pair(last, other, halves[h])
        project(half_z, other, halves[h])
        scaled = row_scale(h)
        for head in range(2):
            kv[h, 0, :, heads[head]] = rotated(1, h, head, scaled)
        go(kv_copy(h, 0))
        kv[h, 1] = (acc[2, halves[h]] * scaled).astype(BF)
        go(kv_copy(h, 1))
        for head in range(2):
            qr[halves[h], heads[head]] = rotated(0, h, head, scaled)

    score_scale = 1.0 / math.sqrt(HD)
    tops, sums, outs = [], [], []
    for head in range(2):
        q = qr[:, heads[head]]
        logits = []
        for h in range(2):
            value = dot(q, kv[h, 0, :, heads[head]], (1, 1)) * score_scale
            logits.append(jnp.where(causal[:, h * half : (h + 1) * half], value, -1e30))
        top = jnp.maximum(*(jnp.max(value, axis=1, keepdims=True) for value in logits))
        expos = [jnp.exp(value - top) for value in logits]
        tops.append(top)
        sums.append(sum(jnp.sum(expo, axis=1, keepdims=True) for expo in expos))
        outs.append(sum(dot(expos[h].astype(BF), kv[h, 1, :, heads[head]]) for h in range(2)))
    for h in range(2):
        kv_copy(h, 0).wait_recv()
        weights = []
        for head in range(2):
            logits = dot(qr[:, heads[head]], kvp[h, 0, :, heads[head]], (1, 1)) * score_scale
            logits = jnp.where(block > 0, logits, -1e30)
            top = jnp.maximum(tops[head], jnp.max(logits, axis=1, keepdims=True))
            expo = jnp.exp(logits - top)
            old = jnp.exp(tops[head] - top)
            tops[head] = top
            sums[head] = sums[head] * old + jnp.sum(expo, axis=1, keepdims=True)
            outs[head] = outs[head] * old
            weights.append(expo.astype(BF))
        kv_copy(h, 1).wait_recv()
        for head in range(2):
            outs[head] = outs[head] + dot(weights[head], kvp[h, 1, :, heads[head]])
    for head in range(2):
        out_ref[1, :, heads[head]] = (outs[head] / sums[head]).astype(BF)

    for copy in sent:
        copy.wait_send()
    for k in range(1, ny):
        pl.when(y < ny - k)(lambda k=k: to_y(k).wait_send())


def tables(tok, blocks):
    freq = 500000.0 ** (-(np.arange(HD // 2) * 2.0 / HD))
    freq = np.concatenate([freq, freq])
    near = np.arange(tok)[:, None] * freq
    far = (np.arange(blocks) * tok)[:, None] * freq
    return tuple(np.stack([np.cos(a), np.sin(a)]).astype(np.float32) for a in (near, far))


def local(sizes, lin_qkv, resid, w_out, w_qkv):
    ny, nx, nz = sizes
    tok, width = resid.shape
    half_z = nz // 2
    near, far = tables(tok, ny * nx)
    scale = 1.0 / math.sqrt(HD * tok * ny * nx)
    rows = 2 * HD // nx
    anywhere = pl.BlockSpec(memory_space=pltpu.HBM)
    dma = pltpu.SemaphoreType.DMA
    vmem = pltpu.VMEM
    scratch = [
        vmem((3, tok, width), BF),
        vmem((tok, width), BF),
        vmem((nz, 2, width, width), BF),
        vmem((3, 2 * nz * width, width), BF),
        vmem(near.shape, F32),
        vmem(far.shape, F32),
        vmem((nx, rows, HD), BF),
        vmem((nx, rows, HD), BF),
        vmem((ny, rows, HD), BF),
        vmem((nx, rows, HD), BF),
        vmem((nx, rows, HD), BF),
        vmem((nx, rows, HD), BF),
        vmem((tok, width), BF),
        vmem((tok, width), F32),
        vmem((tok, width), F32),
        vmem((2, tok, width), BF),
        vmem((nz, tok, width), F32),
        vmem((half_z, PIECES, tok // PIECES, width), BF),
        vmem((half_z, PIECES, tok // PIECES, width), BF),
        vmem((half_z, PIECES, tok // PIECES, width), BF),
        vmem((half_z, PIECES, tok // PIECES, width), BF),
        vmem((PIECES, tok // PIECES, width), BF),
        vmem((PIECES, tok // PIECES, width), BF),
        vmem((nz, 2, tok, width), BF),
        vmem((3, tok, width), F32),
        vmem((tok, HD), F32),
        vmem((2, 2, tok // 2, width), BF),
        vmem((2, 2, tok // 2, width), BF),
        vmem((tok, width), BF),
        dma((5,)),
        dma((nz,)),
        dma((nz,)),
        dma((nz,)),
        dma((nx,)),
        dma((nx,)),
        dma((ny,)),
        dma((ny,)),
        dma((nx,)),
        dma((nx,)),
        dma((nx,)),
        dma((nx,)),
        dma,
        dma,
        dma,
        dma,
        dma((half_z, PIECES)),
        dma((half_z, PIECES)),
        dma((half_z, PIECES)),
        dma((half_z, PIECES)),
        dma((PIECES,)),
        dma((PIECES,)),
        dma((half_z, PIECES)),
        dma((half_z, PIECES)),
        dma((half_z, PIECES)),
        dma((half_z, PIECES)),
        dma((nz, PIECES)),
        dma((nz, PIECES)),
        dma((2, 2)),
        dma((2, 2)),
    ]
    operands = (
        jnp.transpose(lin_qkv, (1, 0, 2)),
        resid,
        w_out,
        jnp.transpose(w_qkv, (1, 0, 2)),
        jnp.asarray(near),
        jnp.asarray(far),
    )
    both = pl.pallas_call(
        functools.partial(layer_pair, sizes, scale),
        name="layer_pair",
        out_shape=jax.ShapeDtypeStruct((2, tok, width), BF),
        in_specs=[anywhere] * 6,
        out_specs=pl.BlockSpec(memory_space=pltpu.VMEM),
        scratch_shapes=scratch,
        compiler_params=pltpu.CompilerParams(
            collective_id=0, has_side_effects=True, vmem_limit_bytes=48 * 1024 * 1024
        ),
    )(
        *(pltpu.with_memory_space_constraint(array, pltpu.HBM) for array in operands)
    )
    return both[0], both[1]


def on_torus(devices, sizes):
    finer = Mesh(devices.reshape(*sizes, 2), ("y", "x", "z", "c"))
    seq, head = ("y", "x"), ("z", "c")
    return jax.shard_map(
        functools.partial(local, sizes),
        mesh=finer,
        in_specs=(P(seq, None, head), P(seq, head), P(head, None), P(None, None, head)),
        out_specs=(P(seq, head), P(seq, head)),
        check_vma=False,
    )


def solution(mesh):
    side = math.isqrt(mesh.shape["seq"])
    return on_torus(mesh.devices, (side, side, mesh.shape["head"] // 2))
```
